32 devices in a mesh: replica: 8 (over y, x, core), shard: 4 (over z).
Axes of the slice: x: 2, y: 2, z: 4, core: 2. Of those that a mesh axis runs over, the one named last changes fastest.
Arguments:
- tokens: bfloat16 [64, 197, 768], P(('replica', 'shard')), may hold values from -6 to 6
- expert_ids: int32 [64, 197, 2], P(('replica', 'shard')), may hold values from 0 to 3, all different within a row; in each aligned block of 394 rows (0 to 393, 394 to 787, ..., all dimensions but the last counted through in order) at most 264 rows name the same one
- qkv_weight: bfloat16 [3, 768, 2304], P(None, 'shard'), may hold values from -0.21875 to 0.21875
- out_weight: bfloat16 [3, 768, 768], P(None, 'shard'), may hold values from -0.875 to 0.875
- router_weight: bfloat16 [3, 768, 4], P(None, 'shard'), may hold values from -0.21875 to 0.21875
- norm_gain: float32 [3, 2, 768], replicated, may hold values from 0.5 to 1.5
- norm_shift: float32 [3, 2, 768], replicated, may hold values from -2 to 2
- expert_in: bfloat16 [3, 4, 768, 3072], P(None, 'shard'), may hold values from -0.21875 to 0.21875
- expert_out: bfloat16 [3, 4, 3072, 768], P(None, 'shard'), may hold values from -0.625 to 0.625
- cotangent: bfloat16 [64, 197, 768], P(('replica', 'shard')), may hold values from -6 to 6
Outputs:
- activations: bfloat16 [64, 197, 768], P(('replica', 'shard'))
- input_grad: float32 [64, 197, 768], P(('replica', 'shard'))
- qkv_grad: float32 [3, 768, 2304], P(None, 'shard')
- out_grad: float32 [3, 768, 768], P(None, 'shard')
- router_grad: float32 [3, 768, 4], P(None, 'shard')
- gain_grad: float32 [3, 2, 768], P(None, None, 'shard')
- shift_grad: float32 [3, 2, 768], P(None, None, 'shard')
- expert_in_grad: float32 [3, 4, 768, 3072], P(None, 'shard', None, 'replica')
- expert_out_grad: float32 [3, 4, 3072, 768], P(None, 'shard', 'replica')
The draws below stay inside these ranges and needn't reach their ends.
Inputs may be any that keep to these rules, and one draw needn't show every extreme that they name: `expert_ids`: the two ids of a token differ. Among the 394 tokens of one device no expert is named more than 264 times, and in every draw some device names some expert exactly 264 times.
All inputs are finite; a program needn't handle non-finite values.
Results may differ from the reference program's by a relative error of at most 0.025.
Values may be sent and summed in bfloat16 or wider, within the bound.
No kernel may reach another device: no remote copies, remote signals or barrier semaphores. Data moves between devices by JAX's collectives and lax.ppermute only.
A program may use at most 384 MiB of HBM per device.

```python
import math
import jax
import jax.numpy as jnp
import numpy as np
from jax import lax

D = 768
HEADS = 12
HEAD = 64
FF = 3072
SEQ = 197
LAYERS = 3
IMG_DEV = 2
EXPERTS = 4
TOK_DEV = 394
IMAGES = 64
CAP = 264


def spiked(entries, stream_key, source, target, blocks, factor):
    owner, partner = [(jnp.arange(entries.shape[axis_at]) // (entries.shape[axis_at] // blocks)).reshape([-1 if axis == axis_at else 1 for axis in range(entries.ndim)]) for axis_at in (source, target)]
    chosen = jax.random.permutation(stream_key, blocks)[partner]
    strong = (owner == chosen) | (owner == (partner + blocks // 2) % blocks)
    return jnp.where(strong, factor * entries, entries)


def steps_of(own_key, dims, shards, least, high):
    gain = 1.0
    for dim, blocks in shards:
        draws = jax.random.uniform(jax.random.fold_in(jax.random.fold_in(own_key, 6), dim), (blocks,), jnp.float32, least / len(shards), high / len(shards))
        gain = gain * jnp.repeat(jnp.exp(draws), dims[dim] // blocks).reshape((-1,) + (1,) * (len(dims) - 1 - dim))
    return gain


def assign_block(rng, own, number, rows, count, top, reach, skew):
    order = jax.random.permutation(rng, count)
    packed, ordinary = load_shares(count, rows * top, reach, skew, True), load_shares(count, rows * top, reach, skew, False)
    places = jnp.arange(count)

    def named(sizes, rotation):
        used = int((sizes > 0).sum())
        fixed = max(1, used // 4)
        moved = fixed + (places - fixed + rotation * (used - fixed)) % max(1, count - fixed)
        return jnp.zeros((count,), jnp.int32).at[order[jnp.where(places < fixed, places, moved)]].set(jnp.asarray(sizes, jnp.int32))

    sizes = jnp.where(number % 4 == 0, named(packed, number // 4), named(ordinary, number - number // 4 - 1))
    mixed = jax.random.permutation(jax.random.fold_in(own, 3), count)
    giver, sink = mixed[0:count // 2 * 2:2], mixed[1:count // 2 * 2:2]
    margin = jnp.minimum(sizes[giver] - 1, reach - sizes[sink]) // 2
    margin = jnp.where((giver == order[0]) | (sink == order[0]) | (sizes[sink] == 0), 0, jnp.maximum(margin, 0))
    moved = jax.random.randint(jax.random.fold_in(own, 4), (count // 2,), 0, 1 << 20) % (margin + 1)
    sizes = sizes.at[giver].add(-moved).at[sink].add(moved)
    labels = jnp.searchsorted(jnp.cumsum(sizes), jnp.arange(rows * top), side="right").astype(jnp.int32)
    table = labels.reshape(top, rows).T
    table = table[jax.random.permutation(jax.random.fold_in(own, 1), rows)]
    rotation = jax.random.randint(jax.random.fold_in(own, 2), (rows, 1), 0, top)
    return jnp.take_along_axis(table, (jnp.arange(top)[None, :] + rotation) % top, axis=1)


def load_shares(count, total, limit, skew, full):
    loads = [(1 << 20) // math.isqrt(rank ** skew) + 1 for rank in range(1, count + 1)]
    largest = limit if full else min(limit, max(-(-total // count), total * loads[0] // sum(loads)))
    least = 1 if total - largest >= count - 1 else 0
    holding, surplus = [largest] + [least] * (count - 1), total - largest - least * (count - 1)
    while surplus > 0:
        free = [i for i in range(1, count) if holding[i] < largest] or [i for i in range(1, count) if holding[i] < limit]
        pool, budget = sum([loads[i] for i in free]), surplus
        for i in free:
            extra = min(limit - holding[i], max(1, budget * loads[i] // pool), surplus)
            holding[i] = holding[i] + extra
            surplus = surplus - extra
    return np.array(holding)


def noise(rng, shape, width, bound, split=(), held_as=jnp.bfloat16):
    drawn = width * jax.random.normal(rng, shape, jnp.float32)
    if split:
        drawn = drawn * steps_of(rng, shape, split, -0.22, 0.18)
    return jnp.clip(drawn, -bound, bound).astype(held_as)


def gaussian_with(key, shape, deviation, reach, split, heavy, held_as=jnp.bfloat16):
    drawn = deviation * jax.random.normal(key, shape, jnp.float32)
    if split:
        drawn = drawn * steps_of(key, shape, split, -0.22, 0.18)
    return jnp.clip(spiked(drawn, jax.random.fold_in(key, 3), *heavy), -reach, reach).astype(held_as)


def setup_inputs(seed: int = 0) -> dict:
    arg_keys = jax.random.split(jax.random.key(seed), 11)
    tokens = noise(arg_keys[0], (IMAGES, SEQ, D), 1.0, 6.0, ((0, 32),))
    expert_ids_keys = jax.random.split(jax.random.fold_in(arg_keys[1], 1), IMAGES * SEQ // TOK_DEV)
    expert_ids_turns = jax.random.permutation(jax.random.fold_in(arg_keys[1], 3), IMAGES * SEQ // TOK_DEV)
    expert_ids = jax.vmap(lambda own, number: assign_block(jax.random.fold_in(arg_keys[1], 2), own, number, TOK_DEV, EXPERTS, 2, CAP, 2))(expert_ids_keys, expert_ids_turns).reshape((IMAGES, SEQ, 2))
    qkv_weight = noise(arg_keys[2], (LAYERS, D, 3 * D), D ** -0.5, 0.21875, ((1, 4),))
    out_weight = noise(arg_keys[3], (LAYERS, D, D), (D // 16) ** -0.5, 0.875, ((1, 4),))
    router_weight = noise(arg_keys[4], (LAYERS, D, EXPERTS), D ** -0.5, 0.21875, ((1, 4),))
    norm_gain = jnp.clip(1.0 + 0.1 * jax.random.normal(arg_keys[5], (LAYERS, 2, D), jnp.float32), 0.5, 1.5)
    norm_shift = noise(arg_keys[6], (LAYERS, 2, D), 0.3, 2.0, (), jnp.float32)
    expert_in = noise(arg_keys[7], (LAYERS, EXPERTS, D, FF), D ** -0.5, 0.21875, ((1, 4),))
    expert_out = noise(arg_keys[8], (LAYERS, EXPERTS, FF, D), (FF // 32) ** -0.5, 0.625, ((1, 4),))
    cotangent = gaussian_with(arg_keys[9], (IMAGES, SEQ, D), 1.0, 6.0, ((0, 32),), (0, 2, 32, 2.75))
    return {"tokens": tokens, "expert_ids": expert_ids, "qkv_weight": qkv_weight, "out_weight": out_weight, "router_weight": router_weight, "norm_gain": norm_gain, "norm_shift": norm_shift, "expert_in": expert_in, "expert_out": expert_out, "cotangent": cotangent}


@jax.custom_vjp
def low(v):
    return lax.optimization_barrier(v.astype(jnp.bfloat16)).astype(jnp.float32)

@jax.custom_vjp
def low_back(v):
    return v

def low_keep(v):
    return (low(v), None)

def low_pass(kept, grad):
    return (grad,)

def back_keep(v):
    return (v, None)

def back_low(kept, grad):
    return (low(grad),)
low.defvjp(low_keep, low_pass)
low_back.defvjp(back_keep, back_low)
eps_norm = 1e-06
highest = lax.Precision.HIGHEST

def norm_rows(values_in, gain_row, shift_row):
    average = lax.optimization_barrier(jnp.mean(values_in, axis=-1, keepdims=True))
    centred = values_in - average
    variance = lax.optimization_barrier(jnp.mean(centred * centred, axis=-1, keepdims=True))
    return centred * lax.rsqrt(variance + eps_norm) * gain_row + shift_row

def slot_positions(block_ids, expert_count, slot_count):
    flat_ids = block_ids.reshape(-1).astype(jnp.int32)
    member = (flat_ids[:, None] == jnp.arange(expert_count, dtype=jnp.int32)[None, :]).astype(jnp.int32)
    earlier = jnp.cumsum(member, axis=0) - member
    return flat_ids * slot_count + lax.optimization_barrier(jnp.sum(earlier * member, axis=1))

def expert_apply(pieces):
    slot_rows, first_weight, second_weight = pieces
    pre_act = low_back(jnp.einsum('ncd,df->ncf', slot_rows, first_weight, precision=highest))
    activated = low(jax.nn.gelu(pre_act, approximate=False))
    return low_back(low(jnp.einsum('ncf,fd->ncd', activated, second_weight, precision=highest)))

def layer_forward(residual, expert_ids, positions, gains, shifts, qkv_w, out_w, router_w, first_weight, second_weight):
    images = residual.shape[0]
    devices = positions.shape[0]
    hidden_one = low(norm_rows(residual, gains[0], shifts[0]))
    qkv_rows = low_back(low(jnp.einsum('bsd,de->bse', hidden_one, qkv_w, precision=highest)))
    queries = qkv_rows[:, :, :D].reshape(images, SEQ, HEADS, HEAD)
    key_rows = qkv_rows[:, :, D:2 * D].reshape(images, SEQ, HEADS, HEAD)
    value_rows = qkv_rows[:, :, 2 * D:].reshape(images, SEQ, HEADS, HEAD)
    scores = low_back(jnp.einsum('bqhd,bkhd->bhqk', queries, key_rows, precision=highest) * HEAD ** (-0.5))
    attn_weights = jax.nn.softmax(scores, axis=-1)
    context = low_back(low(jnp.einsum('bhqk,bkhd->bqhd', low(attn_weights), value_rows, precision=highest)))
    branch = low_back(jnp.einsum('bse,ed->bsd', context.reshape(images, SEQ, D), out_w, precision=highest))
    middle = residual + branch
    hidden_two = low(norm_rows(middle, gains[1], shifts[1]))
    logits = low_back(jnp.einsum('bsd,de->bse', hidden_two, router_w, precision=highest))
    router = jax.nn.softmax(logits, axis=-1)
    gate_values = jnp.take_along_axis(router, expert_ids, axis=-1)
    doubled = jnp.repeat(hidden_two.reshape(devices, TOK_DEV, D), 2, axis=1)
    device_rows = jnp.arange(devices, dtype=jnp.int32)[:, None]
    buffer = jnp.zeros((devices, EXPERTS * CAP, D), jnp.float32).at[device_rows, positions].set(doubled)
    buffer = low_back(buffer).reshape(devices, EXPERTS, CAP, D)
    produced = lax.map(jax.checkpoint(expert_apply), (jnp.transpose(buffer, (1, 0, 2, 3)), first_weight, second_weight))
    produced = jnp.transpose(produced, (1, 0, 2, 3)).reshape(devices, EXPERTS * CAP, D)
    picked = jnp.take_along_axis(produced, positions[:, :, None], axis=1).reshape(images, SEQ, 2, D)
    return middle + lax.optimization_barrier(jnp.sum(gate_values[..., None] * picked, axis=2))

def reference(tokens, expert_ids, qkv_weight, out_weight, router_weight, norm_gain, norm_shift, expert_in, expert_out, cotangent):
    devices = IMAGES // IMG_DEV
    positions = jax.vmap(lambda block_ids: slot_positions(block_ids, EXPERTS, CAP))(expert_ids.reshape(devices, TOK_DEV, 2))

    def forward_pass(residual, qkv_all, out_all, router_all, gain_all, shift_all, first_all, second_all):
        for layer_index in range(LAYERS):
            residual = layer_forward(residual, expert_ids, positions, gain_all[layer_index], shift_all[layer_index], qkv_all[layer_index], out_all[layer_index], router_all[layer_index], first_all[layer_index], second_all[layer_index])
        return residual
    result, pullback = jax.vjp(forward_pass, tokens.astype(jnp.float32), qkv_weight.astype(jnp.float32), out_weight.astype(jnp.float32), router_weight.astype(jnp.float32), norm_gain.astype(jnp.float32), norm_shift.astype(jnp.float32), expert_in.astype(jnp.float32), expert_out.astype(jnp.float32))
    gradients = pullback(cotangent.astype(jnp.float32))
    return (result.astype(jnp.bfloat16), gradients[0], gradients[1], gradients[2], gradients[3], gradients[4], gradients[5], gradients[6], gradients[7])
```

```python
import jax
import jax.numpy as jnp
from jax import lax
from jax.sharding import PartitionSpec as P

HEAD = 64
LAYERS = 3

eps_norm = 1e-06
inv_root_two = 0.7071067811865476
inv_root_two_pi = 0.3989422804014327
bf16 = jnp.bfloat16
f32 = jnp.float32


def norm_parts(values_in):
    average = jnp.mean(values_in, axis=-1, keepdims=True)
    centred = values_in - average
    variance = jnp.mean(centred * centred, axis=-1, keepdims=True)
    inverse = lax.rsqrt(variance + eps_norm)
    return (centred * inverse, inverse)


def norm_back(grad_out, normed, inverse, gain_row):
    scaled = grad_out * gain_row
    inner = jnp.mean(scaled, axis=-1, keepdims=True)
    along = jnp.mean(scaled * normed, axis=-1, keepdims=True)
    grad_in = inverse * (scaled - inner - normed * along)
    return (grad_in, jnp.sum(grad_out * normed, axis=0), jnp.sum(grad_out, axis=0))


def dot_on(left, right, left_axis, right_axis):
    return lax.dot_general(
        left, right, (((left_axis,), (right_axis,)), ((), ())), preferred_element_type=f32
    )


def swap(values, bit):
    count = lax.axis_size("replica")
    return lax.ppermute(values, "replica", [(n, n ^ bit) for n in range(count)])


def bit_of(bit):
    return (lax.axis_index("replica") & bit) != 0


def orders():
    bits = []
    step = 2
    while step < lax.axis_size("replica"):
        bits.append(step)
        step *= 2
    return bits, bits[::-1]


def halve(values, bit, size):
    rows = values.shape[0]
    view = values.reshape((rows // (2 * size), 2, size) + values.shape[1:])
    own = bit_of(bit).astype(jnp.int32)
    kept = lax.dynamic_index_in_dim(view, own, 1, keepdims=False)
    sent = lax.dynamic_index_in_dim(view, 1 - own, 1, keepdims=False)
    return kept.reshape((rows // 2,) + values.shape[1:]), sent.reshape((rows // 2,) + values.shape[1:])


def scatter_replica(values):
    kept, sent = halve(values, 1, 1)
    values = (kept.astype(f32) + swap(sent, 1).astype(f32)).astype(bf16)
    middle = values.shape[-2] // 16 * 8
    parts = []
    for piece, order in zip((values[..., :middle, :], values[..., middle:, :]), orders()):
        for at, bit in enumerate(order):
            size = 1
            for other in order[at + 1 :]:
                if other < bit:
                    size *= 2
            kept, sent = halve(piece, bit, size)
            piece = (kept.astype(f32) + swap(sent, bit).astype(f32)).astype(bf16)
        parts.append(piece[0])
    return parts


def gather_replica(parts):
    done = []
    for piece, order in zip(parts, orders()):
        piece = piece[None]
        held = []
        for bit in order[::-1]:
            size = 1
            for other in held:
                if other < bit:
                    size *= 2
            other_piece = swap(piece, bit)
            rows = piece.shape[0]
            shape = (rows // size, size) + piece.shape[1:]
            mine, theirs = piece.reshape(shape), other_piece.reshape(shape)
            upper = bit_of(bit)
            piece = jnp.stack(
                [jnp.where(upper, theirs, mine), jnp.where(upper, mine, theirs)], axis=1
            ).reshape((2 * rows,) + piece.shape[1:])
            held.append(bit)
        done.append(piece)
    values = jnp.concatenate(done, axis=-2)
    other = swap(values, 1)
    upper = bit_of(1)
    rows = values.shape[0]
    return jnp.stack(
        [jnp.where(upper, other, values), jnp.where(upper, values, other)], axis=1
    ).reshape((2 * rows,) + values.shape[1:])


def gather_dense(packed):
    rows, columns = packed.shape
    count = lax.axis_size("replica")
    width = columns // count
    own = lax.dynamic_slice_in_dim(packed, lax.axis_index("replica") * width, width, axis=1)
    tall = lax.all_gather(own, "shard", axis=0, tiled=True)
    return lax.all_gather(tall, "replica", axis=0, tiled=False)


def reduce_dense(grad_qkv_w, grad_out_w, items):
    features = grad_out_w.shape[0]
    count = lax.axis_size("replica")
    shards_ = lax.axis_size("shard")
    rows = features // shards_
    dense = jnp.concatenate([grad_qkv_w.astype(bf16), grad_out_w.astype(bf16)], axis=1)
    width = dense.shape[1] // count
    chunks = jnp.transpose(dense.reshape(shards_, rows, count, width), (2, 0, 1, 3))
    extra = jnp.zeros((count, shards_, 8, width), bf16)
    small = items.astype(bf16).reshape(items.shape[0], shards_, rows)
    extra = extra.at[: items.shape[0], :, 0, :rows].set(small)
    chunks = jnp.concatenate([chunks, extra], axis=2)
    parts = scatter_replica(chunks)
    whole = jnp.concatenate(parts, axis=-2)
    swapped = lax.all_to_all(whole, "shard", split_axis=0, concat_axis=0, tiled=True)
    total = jnp.sum(swapped.astype(f32), axis=0).astype(bf16)
    middle = total.shape[-2] // 16 * 8
    result = gather_replica([total[:middle], total[middle:]])
    body = jnp.transpose(result[:, :rows], (1, 0, 2)).reshape(rows, count * width)
    return (
        body[:, : 3 * features].astype(f32),
        body[:, 3 * features :].astype(f32),
        result[: items.shape[0], rows, :rows].astype(f32),
    )


def split_heads(qkv_rows, images, length, head_count):
    features = qkv_rows.shape[1] // 3
    head_size = features // head_count
    queries = qkv_rows[:, :features].reshape(images, length, head_count, head_size)
    key_rows = qkv_rows[:, features : 2 * features].reshape(images, length, head_count, head_size)
    value_rows = qkv_rows[:, 2 * features :].reshape(images, length, head_count, head_size)
    return (queries, key_rows, value_rows)


def attend(queries, key_rows):
    scores = jnp.einsum(
        "bqhd,bkhd->bhqk", queries, key_rows, preferred_element_type=f32
    ) * queries.shape[-1] ** (-0.5)
    highest = jnp.max(scores, axis=-1, keepdims=True)
    raised = jnp.exp(scores - highest)
    row_total = jnp.sum(raised, axis=-1, keepdims=True)
    return (raised / row_total, highest + jnp.log(row_total))


def exchange(rows, experts):
    shape = rows.shape
    blocks = rows.reshape(experts, shape[0] // experts, shape[1])
    return lax.all_to_all(blocks, "shard", split_axis=0, concat_axis=0, tiled=True).reshape(shape)


def forward_layer(
    residual, qkv_w, out_w, router_t, gains, shifts, first_weight, second_weight, choose, places, info
):
    images, length, head_count, experts = info
    token_count, features = residual.shape
    normed_one, inverse_one = norm_parts(residual)
    hidden_one = (normed_one * gains[0] + shifts[0]).astype(bf16)
    qkv_rows = jnp.dot(hidden_one, qkv_w, preferred_element_type=f32).astype(bf16)
    queries, key_rows, value_rows = split_heads(qkv_rows, images, length, head_count)
    attn_weights, log_total = attend(queries, key_rows)
    context = (
        jnp.einsum(
            "bhqk,bkhd->bqhd", attn_weights.astype(bf16), value_rows, preferred_element_type=f32
        )
        .astype(bf16)
        .reshape(token_count, features)
    )
    middle = residual + jnp.dot(context, out_w, preferred_element_type=f32)
    normed_two, inverse_two = norm_parts(middle)
    hidden_two = (normed_two * gains[1] + shifts[1]).astype(bf16)
    router = jax.nn.softmax(dot_on(hidden_two, router_t, 1, 1), axis=-1)
    gates = [jnp.sum(choose[k] * router, axis=1, keepdims=True) for k in range(2)]
    both, singles = places
    arrived = exchange(dot_on(both, hidden_two, 0, 0).astype(bf16), experts)
    pre_act = jnp.dot(arrived, first_weight, preferred_element_type=f32)
    spread = lax.erf(pre_act * inv_root_two)
    activated = (0.5 * pre_act * (1.0 + spread)).astype(bf16)
    slope = (
        0.5 * (1.0 + spread) + pre_act * jnp.exp(-0.5 * pre_act * pre_act) * inv_root_two_pi
    ).astype(bf16)
    produced = jnp.dot(activated, second_weight, preferred_element_type=f32).astype(bf16)
    returned = exchange(produced, experts)
    picked = [jnp.dot(singles[k], returned, preferred_element_type=f32) for k in range(2)]
    residual_next = middle + (gates[0] * picked[0] + gates[1] * picked[1])
    picked = [p.astype(bf16) for p in picked]
    record = (
        normed_one, inverse_one, hidden_one, qkv_rows, log_total, context, normed_two, inverse_two,
        hidden_two, router, gates, arrived, slope, activated, picked,
    )
    return (record, residual_next)


def backward_layer(
    gradient, record, qkv_w, out_w, router_t, gains, first_weight, second_weight, choose, places, info
):
    images, length, head_count, experts = info
    (
        normed_one, inverse_one, hidden_one, qkv_rows, log_total, context, normed_two, inverse_two,
        hidden_two, router, gates, arrived, slope, activated, picked,
    ) = record
    both, singles = places
    token_count, features = gradient.shape
    grad_slots = dot_on(singles[0], (gates[0] * gradient).astype(bf16), 0, 0) + dot_on(
        singles[1], (gates[1] * gradient).astype(bf16), 0, 0
    )
    grad_arrived = exchange(grad_slots.astype(bf16), experts)
    grad_act = dot_on(grad_arrived, second_weight, 1, 1)
    grad_pre = (grad_act * slope.astype(f32)).astype(bf16)
    grad_rows = dot_on(grad_pre, first_weight, 1, 1).astype(bf16)
    grad_back = exchange(grad_rows, experts)
    expert_terms = jnp.concatenate(
        [dot_on(grad_pre, arrived, 0, 0).astype(bf16), dot_on(activated, grad_arrived, 0, 0).astype(bf16)],
        axis=1,
    )
    grad_router = sum(
        choose[k] * jnp.sum(gradient * picked[k].astype(f32), axis=1, keepdims=True) for k in range(2)
    )
    grad_logits = (
        router * (grad_router - jnp.sum(router * grad_router, axis=-1, keepdims=True))
    ).astype(bf16)
    grad_router_w = dot_on(grad_logits, hidden_two, 0, 0)
    grad_two = jnp.dot(both, grad_back, preferred_element_type=f32) + jnp.dot(
        grad_logits, router_t, preferred_element_type=f32
    )
    grad_norm_two, gain_two, shift_two = norm_back(grad_two, normed_two, inverse_two, gains[1])
    grad_middle = gradient + grad_norm_two
    grad_attn = grad_middle.astype(bf16)
    grad_out_w = dot_on(context, grad_attn, 0, 0)
    queries, key_rows, value_rows = split_heads(qkv_rows, images, length, head_count)
    grad_context = dot_on(grad_attn, out_w, 1, 1).astype(bf16).reshape(queries.shape)
    score_scale = queries.shape[-1] ** (-0.5)
    scores = (
        jnp.einsum("bqhd,bkhd->bhqk", queries, key_rows, preferred_element_type=f32) * score_scale
    )
    attn_weights = jnp.exp(scores - log_total)
    grad_weights = jnp.einsum(
        "bqhd,bkhd->bhqk", grad_context, value_rows, preferred_element_type=f32
    )
    grad_values = jnp.einsum(
        "bhqk,bqhd->bkhd", attn_weights.astype(bf16), grad_context, preferred_element_type=f32
    )
    grad_scores = (
        attn_weights * (grad_weights - jnp.sum(attn_weights * grad_weights, axis=-1, keepdims=True))
    ).astype(bf16)
    grad_queries = (
        jnp.einsum("bhqk,bkhd->bqhd", grad_scores, key_rows, preferred_element_type=f32) * score_scale
    )
    grad_keys = (
        jnp.einsum("bhqk,bqhd->bkhd", grad_scores, queries, preferred_element_type=f32) * score_scale
    )
    grad_qkv = jnp.concatenate(
        [
            grad_queries.reshape(token_count, features),
            grad_keys.reshape(token_count, features),
            grad_values.reshape(token_count, features),
        ],
        axis=1,
    ).astype(bf16)
    grad_qkv_w = dot_on(hidden_one, grad_qkv, 0, 0)
    grad_one = dot_on(grad_qkv, qkv_w, 1, 1)
    grad_norm_one, gain_one, shift_one = norm_back(grad_one, normed_one, inverse_one, gains[0])
    items = jnp.concatenate(
        [grad_router_w, jnp.stack([gain_one, gain_two, shift_one, shift_two])], axis=0
    )
    return (grad_middle + grad_norm_one, (grad_qkv_w, grad_out_w, items), expert_terms)


def shards(
    tokens, expert_ids, qkv_weight, out_weight, router_weight, norm_gain, norm_shift, expert_in,
    expert_out, cotangent,
):
    images, length, features = tokens.shape
    token_count = images * length
    head_count = features // HEAD
    experts = lax.axis_size("shard")
    capacity = (8 * token_count + 24 * experts - 1) // (24 * experts) * 8
    slots = experts * capacity
    packed = jnp.concatenate([qkv_weight, out_weight], axis=2)
    gathered = [gather_dense(packed[index]) for index in range(LAYERS)]
    router_all = lax.all_gather(
        jnp.transpose(router_weight, (0, 2, 1)).reshape(LAYERS * experts, -1), "shard", axis=1, tiled=True
    ).reshape(LAYERS, experts, features)
    ids_pair = expert_ids.reshape(token_count, 2)
    ids_flat = ids_pair.reshape(-1)
    labels = jnp.arange(experts, dtype=jnp.int32)
    member = (ids_flat[:, None] == labels[None, :]).astype(jnp.int32)
    earlier = jnp.cumsum(member, axis=0) - member
    positions = (ids_flat * capacity + jnp.sum(earlier * member, axis=1)).reshape(token_count, 2)
    choose = [(ids_pair[:, k : k + 1] == labels[None, :]).astype(f32) for k in range(2)]
    slot_row = jnp.arange(slots, dtype=jnp.int32)[None, :]
    singles = [(positions[:, k : k + 1] == slot_row).astype(bf16) for k in range(2)]
    places = (singles[0] + singles[1], singles)
    info = (images, length, head_count, experts)
    residual = tokens.reshape(token_count, features).astype(f32)
    records = []
    weights = []
    for index in range(LAYERS):
        whole = jnp.transpose(gathered[index], (1, 0, 2)).reshape(features, 4 * features)
        dense_set = (whole[:, : 3 * features], whole[:, 3 * features :], router_all[index])
        weights.append(dense_set)
        record, residual = forward_layer(
            residual, *dense_set, norm_gain[index], norm_shift[index], expert_in[index, 0],
            expert_out[index, 0], choose, places, info,
        )
        records.append(record)
    activations = residual.astype(bf16).reshape(images, length, features)
    gradient = cotangent.reshape(token_count, features).astype(f32)
    dense_out = [None] * LAYERS
    expert_sums = [None] * LAYERS
    for index in range(LAYERS - 1, -1, -1):
        gradient, dense_terms, expert_terms = backward_layer(
            gradient, records[index], *weights[index], norm_gain[index], expert_in[index, 0],
            expert_out[index, 0], choose, places, info,
        )
        expert_sums[index] = lax.psum_scatter(
            expert_terms, "replica", scatter_dimension=0, tiled=True
        )
        dense_out[index] = reduce_dense(*dense_terms)
    input_grad = gradient.reshape(images, length, features)
    qkv_grad = jnp.stack([dense_out[index][0] for index in range(LAYERS)])
    out_grad = jnp.stack([dense_out[index][1] for index in range(LAYERS)])
    items = jnp.stack([dense_out[index][2] for index in range(LAYERS)])
    router_grad = jnp.transpose(items[:, :experts], (0, 2, 1))
    gain_grad = items[:, experts : experts + 2]
    shift_grad = items[:, experts + 2 :]
    expert_in_grad = jnp.stack(
        [jnp.transpose(expert_sums[index][:, :features].astype(f32))[None] for index in range(LAYERS)]
    )
    expert_out_grad = jnp.stack(
        [expert_sums[index][:, features:].astype(f32)[None] for index in range(LAYERS)]
    )
    return (
        activations, input_grad, qkv_grad, out_grad, router_grad, gain_grad, shift_grad,
        expert_in_grad, expert_out_grad,
    )


def solution(mesh):
    in_specs = (
        P(("replica", "shard"), None, None),
        P(("replica", "shard"), None, None),
        P(None, "shard", None),
        P(None, "shard", None),
        P(None, "shard", None),
        P(),
        P(),
        P(None, "shard", None, None),
        P(None, "shard", None, None),
        P(("replica", "shard"), None, None),
    )
    out_specs = (
        P(("replica", "shard"), None, None),
        P(("replica", "shard"), None, None),
        P(None, "shard", None),
        P(None, "shard", None),
        P(None, "shard", None),
        P(None, None, "shard"),
        P(None, None, "shard"),
        P(None, "shard", None, "replica"),
        P(None, "shard", "replica", None),
    )
    return jax.shard_map(shards, mesh=mesh, in_specs=in_specs, out_specs=out_specs, check_vma=False)
```

```python
import functools

import jax
import jax.numpy as jnp
from jax import lax
from jax.experimental import pallas as pl
from jax.experimental.pallas import tpu as pltpu
from jax.sharding import PartitionSpec as P

HEAD = 64
LAYERS = 3

eps_norm = 1e-06
inv_root_two = 0.7071067811865476
inv_root_two_pi = 0.3989422804014327
bf16 = jnp.bfloat16
f32 = jnp.float32


def dot_on(left, right, left_axis, right_axis):
    return lax.dot_general(
        left, right, (((left_axis,), (right_axis,)), ((), ())), preferred_element_type=f32
    )


def swap(values, axis, bit):
    count = lax.axis_size(axis)
    return lax.ppermute(values, axis, [(n, n ^ bit) for n in range(count)])


def bit_of(axis, bit):
    return (lax.axis_index(axis) & bit) != 0


def bits_from(axis, step):
    bits = []
    while step < lax.axis_size(axis):
        bits.append(step)
        step *= 2
    return bits


def orders():
    bits = bits_from("replica", 2)
    return bits, bits[::-1]


def add_swapped(values, axis, bit, size, at):
    lead, rows, rest = values.shape[:at], values.shape[at], values.shape[at + 1 :]
    view = values.reshape(lead + (rows // (2 * size), 2, size) + rest)
    own = bit_of(axis, bit).astype(jnp.int32)
    kept = lax.dynamic_index_in_dim(view, own, at + 1, keepdims=False)
    sent = lax.dynamic_index_in_dim(view, 1 - own, at + 1, keepdims=False)
    shape = lead + (rows // 2,) + rest
    arrived = swap(sent.reshape(shape), axis, bit)
    return (kept.reshape(shape).astype(f32) + arrived.astype(f32)).astype(bf16)


def join_swapped(values, axis, bit, size, at):
    other = swap(values, axis, bit)
    lead, rows, rest = values.shape[:at], values.shape[at], values.shape[at + 1 :]
    shape = lead + (rows // size, size) + rest
    mine, theirs = values.reshape(shape), other.reshape(shape)
    upper = bit_of(axis, bit)
    pair = [jnp.where(upper, theirs, mine), jnp.where(upper, mine, theirs)]
    return jnp.stack(pair, axis=at + 1).reshape(lead + (2 * rows,) + rest)


def size_below(bit, held):
    size = 1
    for other in held:
        if other < bit:
            size *= 2
    return size


def cut(values):
    middle = values.shape[-2] // 16 * 8
    return (values[..., :middle, :], values[..., middle:, :])


def scatter_replica(values):
    values = add_swapped(values, "replica", 1, 1, 1)
    parts = []
    for piece, order in zip(cut(values), orders()):
        for at, bit in enumerate(order):
            piece = add_swapped(piece, "replica", bit, size_below(bit, order[at + 1 :]), 1)
        parts.append(piece[:, 0])
    return jnp.concatenate(parts, axis=-2)


def gather_replica(values):
    done = []
    for piece, order in zip(cut(values), orders()):
        piece = piece[:, None]
        held = []
        for bit in order[::-1]:
            piece = join_swapped(piece, "replica", bit, size_below(bit, held), 1)
            held.append(bit)
        done.append(piece)
    return join_swapped(jnp.concatenate(done, axis=-2), "replica", 1, 1, 1)


def after(values, *others):
    return lax.optimization_barrier((values,) + others)[0]


def gather_shard(packed):
    rows, columns = packed.shape
    width = columns // lax.axis_size("replica")
    own = lax.dynamic_slice_in_dim(packed, lax.axis_index("replica") * width, width, axis=1)
    shards_ = lax.axis_size("shard")
    spread = jnp.broadcast_to(own[None], (shards_, rows, width))
    tall = lax.all_to_all(spread, "shard", split_axis=0, concat_axis=0, tiled=True)
    return tall.reshape(shards_ * rows, width)


def reduce_tail(chunks):
    whole = scatter_replica(chunks[None])[0]
    for bit in bits_from("shard", 1)[::-1]:
        whole = add_swapped(whole, "shard", bit, bit, 0)
    return gather_replica(whole)[0]


def norm_rows_of(values, features):
    average = jnp.sum(values, axis=-1, keepdims=True) * (1.0 / features)
    centred = values - average
    variance = jnp.sum(centred * centred, axis=-1, keepdims=True) * (1.0 / features)
    inverse = lax.rsqrt(variance + eps_norm)
    return centred * inverse, inverse


def soft_scores(queries, key_rows, length):
    scores = dot_on(queries, key_rows, 1, 1) * HEAD ** (-0.5)
    column = lax.broadcasted_iota(jnp.int32, scores.shape, 1)
    scores = jnp.where(column < length, scores, -1e30)
    raised = jnp.exp(scores - jnp.max(scores, axis=-1, keepdims=True))
    return raised * (1.0 / jnp.sum(raised, axis=-1, keepdims=True))


def attention_kernel(length, res_ref, w_ref, rt_ref, gain_ref, shift_ref, qkv_ref, ctx_ref, mid_ref, hid_ref, log_ref):
    residual = res_ref[0]
    features = residual.shape[1]
    normed, _ = norm_rows_of(residual, features)
    hidden = (normed * gain_ref[0:1] + shift_ref[0:1]).astype(bf16)
    width = w_ref.shape[2]
    inner = 3 * features // width
    for chunk in range(inner):
        qkv_ref[0, :, chunk * width : (chunk + 1) * width] = jnp.dot(
            hidden, w_ref[chunk], preferred_element_type=f32
        ).astype(bf16)
    for pair in range(features // (2 * HEAD)):
        outs = []
        for head in (2 * pair, 2 * pair + 1):
            at = head * HEAD
            queries, key_rows, value_rows = [
                qkv_ref[0, :, part * features + at : part * features + at + HEAD] for part in range(3)
            ]
            weights = soft_scores(queries, key_rows, length).astype(bf16)
            outs.append(jnp.dot(weights, value_rows, preferred_element_type=f32).astype(bf16))
        ctx_ref[0, :, 2 * pair * HEAD : (2 * pair + 2) * HEAD] = jnp.concatenate(outs, axis=1)
    for chunk in range(inner, w_ref.shape[0]):
        at = (chunk - inner) * width
        mid_ref[0, :, at : at + width] = res_ref[0, :, at : at + width] + jnp.dot(
            ctx_ref[0], w_ref[chunk], preferred_element_type=f32
        )
    middle = mid_ref[0]
    normed, _ = norm_rows_of(middle, features)
    hidden = (normed * gain_ref[1:2] + shift_ref[1:2]).astype(bf16)
    hid_ref[0] = hidden
    log_ref[0] = dot_on(hidden, rt_ref[...], 1, 1)


def attention_forward(residual, weight, router_t, gains, shifts, length):
    images, rows, features = residual.shape

    def per_image(width):
        return pl.BlockSpec((1, rows, width), lambda n: (n, 0, 0))

    def whole(shape):
        return pl.BlockSpec(shape, lambda n: (0,) * len(shape), pipeline_mode=pl.Buffered(1))

    extra = router_t.shape[0]
    shape = jax.ShapeDtypeStruct
    return pl.pallas_call(
        functools.partial(attention_kernel, length),
        grid=(images,),
        in_specs=[
            per_image(features), whole(weight.shape), whole(router_t.shape), whole(gains.shape),
            whole(shifts.shape),
        ],
        out_specs=[
            per_image(3 * features), per_image(features), per_image(features), per_image(features),
            per_image(extra),
        ],
        out_shape=[
            shape((images, rows, 3 * features), bf16), shape((images, rows, features), bf16),
            shape((images, rows, features), f32), shape((images, rows, features), bf16),
            shape((images, rows, extra), f32),
        ],
        compiler_params=pltpu.CompilerParams(
            dimension_semantics=("arbitrary",), vmem_limit_bytes=48 * 2**20
        ),
        name="attention_forward",
    )(residual, weight, router_t, gains, shifts)


def norm_back_rows(grad_out, normed, inverse, gain_row, features):
    scaled = grad_out * gain_row
    inner = jnp.sum(scaled, axis=-1, keepdims=True) * (1.0 / features)
    along = jnp.sum(scaled * normed, axis=-1, keepdims=True) * (1.0 / features)
    grad_in = inverse * (scaled - inner - normed * along)
    gain_sum = jnp.sum(grad_out * normed, axis=0, keepdims=True)
    return grad_in, gain_sum, jnp.sum(grad_out, axis=0, keepdims=True)


def attention_back_kernel(
    length, two_ref, grad_ref, res_ref, mid_ref, qkv_ref, ctx_ref, w_ref, gain_ref, shift_ref,
    in_ref, dw_ref, norm_ref, dqkv_ref, sum_ref, norm_sum_ref,
):
    step = pl.program_id(0)
    features = res_ref.shape[2]
    scale = HEAD ** (-0.5)

    @pl.when(step == 0)
    def _():
        sum_ref[...] = jnp.zeros_like(sum_ref)
        norm_sum_ref[...] = jnp.zeros_like(norm_sum_ref)

    normed, inverse = norm_rows_of(mid_ref[0], features)
    grad_in, gain_two, shift_two = norm_back_rows(two_ref[0], normed, inverse, gain_ref[1:2], features)
    grad_middle = grad_ref[0] + grad_in
    in_ref[0] = grad_middle
    grad_attn = grad_middle.astype(bf16)
    width = w_ref.shape[2]
    inner_chunks = 3 * features // width
    grad_context = jnp.zeros(grad_attn.shape, f32)
    for chunk in range(inner_chunks, w_ref.shape[0]):
        at = (chunk - inner_chunks) * width
        part = grad_attn[:, at : at + width]
        sum_ref[chunk] += dot_on(ctx_ref[0], part, 0, 0)
        grad_context += dot_on(part, w_ref[chunk], 1, 1)
    grad_context = grad_context.astype(bf16)
    for pair in range(features // (2 * HEAD)):
        outs = ([], [], [])
        for head in (2 * pair, 2 * pair + 1):
            at = head * HEAD
            queries, key_rows, value_rows = [
                qkv_ref[0, :, part * features + at : part * features + at + HEAD] for part in range(3)
            ]
            grad_head = grad_context[:, at : at + HEAD]
            weights = soft_scores(queries, key_rows, length)
            grad_weights = dot_on(grad_head, value_rows, 1, 1)
            outs[2].append(dot_on(weights.astype(bf16), grad_head, 0, 0))
            inner = jnp.sum(weights * grad_weights, axis=-1, keepdims=True)
            grad_scores = (weights * (grad_weights - inner)).astype(bf16)
            outs[0].append(jnp.dot(grad_scores, key_rows, preferred_element_type=f32) * scale)
            outs[1].append(dot_on(grad_scores, queries, 0, 0) * scale)
        for part in range(3):
            at = part * features + 2 * pair * HEAD
            dqkv_ref[:, at : at + 2 * HEAD] = jnp.concatenate(outs[part], axis=1).astype(bf16)
    normed, inverse = norm_rows_of(res_ref[0], features)
    hidden = (normed * gain_ref[0:1] + shift_ref[0:1]).astype(bf16)
    grad_one = jnp.zeros(normed.shape, f32)
    for chunk in range(inner_chunks):
        part = dqkv_ref[:, chunk * width : (chunk + 1) * width]
        sum_ref[chunk] += dot_on(hidden, part, 0, 0)
        grad_one += dot_on(part, w_ref[chunk], 1, 1)
    grad_in, gain_one, shift_one = norm_back_rows(grad_one, normed, inverse, gain_ref[0:1], features)
    in_ref[0] += grad_in
    for row, value in enumerate((gain_one, gain_two, shift_one, shift_two)):
        norm_sum_ref[row : row + 1] += value

    @pl.when(step == pl.num_programs(0) - 1)
    def _():
        dw_ref[...] = sum_ref[...].astype(bf16)
        norm_ref[...] = norm_sum_ref[...]


def attention_backward(grad_two, gradient, residual, middle, qkv_rows, context, weight, gains, shifts, length):
    images, rows, features = residual.shape

    def per_image(width):
        return pl.BlockSpec((1, rows, width), lambda n: (n, 0, 0))

    def whole(shape):
        return pl.BlockSpec(shape, lambda n: (0,) * len(shape), pipeline_mode=pl.Buffered(1))

    shape = jax.ShapeDtypeStruct
    return pl.pallas_call(
        functools.partial(attention_back_kernel, length),
        grid=(images,),
        in_specs=[per_image(features)] * 4
        + [per_image(3 * features), per_image(features), whole(weight.shape), whole(gains.shape),
           whole(shifts.shape)],
        out_specs=[per_image(features), whole(weight.shape), whole((8, features))],
        out_shape=[
            shape((images, rows, features), f32), shape(weight.shape, bf16),
            shape((8, features), f32),
        ],
        scratch_shapes=[
            pltpu.VMEM((rows, 3 * features), bf16), pltpu.VMEM(weight.shape, f32),
            pltpu.VMEM((8, features), f32),
        ],
        compiler_params=pltpu.CompilerParams(
            dimension_semantics=("arbitrary",), vmem_limit_bytes=56 * 2**20
        ),
        name="attention_backward",
    )(grad_two, gradient, residual, middle, qkv_rows, context, weight, gains, shifts)


def expert_grads(terms):
    pres, arrived, acts, grads = terms
    groups = len(pres)
    hidden = pres[0].shape[1]
    features = arrived[0].shape[1]
    count = lax.axis_size("replica")
    per = hidden // count
    block = max(per, 384)

    def kernel(*refs):
        out_ref = refs[-1]
        parts = [refs[n * groups : (n + 1) * groups] for n in range(4)]
        for side, (left, right) in enumerate((parts[:2], parts[2:])):
            total = dot_on(left[0][...], right[0][...], 0, 0)
            for n in range(1, groups):
                total += dot_on(left[n][...], right[n][...], 0, 0)
            for n in range(out_ref.shape[0]):
                out_ref[n, side] = total[n * per : (n + 1) * per].astype(bf16)

    cut_spec = [pl.BlockSpec((v.shape[0], block), lambda n: (0, n)) for v in pres]
    full_spec = [
        pl.BlockSpec(v.shape, lambda n: (0, 0), pipeline_mode=pl.Buffered(1)) for v in arrived
    ]
    return pl.pallas_call(
        kernel,
        grid=(hidden // block,),
        in_specs=cut_spec + full_spec + cut_spec + full_spec,
        out_specs=pl.BlockSpec((block // per, 2, per, features), lambda n: (n, 0, 0, 0)),
        out_shape=jax.ShapeDtypeStruct((count, 2, per, features), bf16),
        compiler_params=pltpu.CompilerParams(
            dimension_semantics=("arbitrary",), vmem_limit_bytes=40 * 2**20
        ),
        name="expert_grads",
    )(*pres, *arrived, *acts, *grads)


def expert_reduce(partial):
    return lax.psum_scatter(
        partial.reshape(-1, partial.shape[-1]), "replica", scatter_dimension=0, tiled=True
    )


def assemble_kernel(features, *refs):
    parts, qkv_ref, out_ref = refs[:-2], refs[-2], refs[-1]
    for layer, part in enumerate(parts):
        width = part.shape[2]
        inner = 3 * features // width
        for chunk in range(part.shape[0]):
            rows = part[chunk].astype(f32)
            if chunk < inner:
                qkv_ref[layer, :, chunk * width : (chunk + 1) * width] = rows
            else:
                at = (chunk - inner) * width
                out_ref[layer, :, at : at + width] = rows


def assemble(parts, features):
    rows = parts[0].shape[1]
    shape = jax.ShapeDtypeStruct
    return pl.pallas_call(
        functools.partial(assemble_kernel, features),
        out_shape=[
            shape((len(parts), rows, 3 * features), f32), shape((len(parts), rows, features), f32)
        ],
        compiler_params=pltpu.CompilerParams(vmem_limit_bytes=40 * 2**20),
        name="assemble",
    )(*parts)


def group_list():
    count = lax.axis_size("shard")
    return [list(range(count // 2)), list(range(count // 2, count))]


def expert_forward(arrived, first_weight, second_weight):
    pre_act = jnp.dot(arrived, first_weight, preferred_element_type=f32)
    spread = lax.erf(pre_act * inv_root_two)
    activated = (0.5 * pre_act * (1.0 + spread)).astype(bf16)
    slope = (
        0.5 * (1.0 + spread) + pre_act * jnp.exp(-0.5 * pre_act * pre_act) * inv_root_two_pi
    ).astype(bf16)
    produced = jnp.dot(activated, second_weight, preferred_element_type=f32).astype(bf16)
    return activated, slope, produced


def forward_layer(
    residual, weight, router_t, gains, shifts, first_weight, second_weight, choose, places, length,
    tall,
):
    images, rows, features = residual.shape
    experts = len(places)
    qkv_rows, context, middle, hidden_two, logits = attention_forward(
        residual, weight, router_t, gains, shifts, length
    )
    gathered = None
    if tall is not None:
        hidden_two, tall = lax.optimization_barrier((hidden_two, tall))
        gathered = lax.all_gather(tall, "replica", axis=0, tiled=False)
    hidden_two = hidden_two.reshape(-1, features)
    router = jax.nn.softmax(logits.reshape(-1, logits.shape[-1])[:, :experts], axis=-1)
    gates = [jnp.sum(choose[k] * router, axis=1, keepdims=True) for k in range(2)]
    record_moe, picked = [], [0.0, 0.0]
    sent = {}
    for j in sorted(places, reverse=True):
        block = dot_on(places[j][0], hidden_two, 0, 0).astype(bf16)
        sent[j] = swap(block, "shard", j) if j else block
    for group in group_list():
        arrived = jnp.concatenate([sent[j] for j in group], axis=0)
        activated, slope, produced = expert_forward(arrived, first_weight, second_weight)
        capacity = produced.shape[0] // len(group)
        back = {}
        for at, j in reversed(list(enumerate(group))):
            block = produced[at * capacity : (at + 1) * capacity]
            back[j] = swap(block, "shard", j) if j else block
        returned = jnp.concatenate([back[j] for j in group], axis=0)
        for k in range(2):
            single = jnp.concatenate([places[j][1][k] for j in group], axis=1)
            picked[k] = picked[k] + jnp.dot(single, returned, preferred_element_type=f32)
        record_moe.append((arrived, slope, activated))
    mixed = gates[0] * picked[0] + gates[1] * picked[1]
    residual_next = middle + mixed.reshape(middle.shape)
    if gathered is not None:
        residual_next, gathered = lax.optimization_barrier((residual_next, gathered))
    picked = [p.astype(bf16) for p in picked]
    record = (
        residual, qkv_rows, context, middle, hidden_two, router, gates, record_moe, picked,
    )
    return (record, residual_next, gathered)


def backward_layer(
    gradient, record, weight, router_t, gains, shifts, first_weight, second_weight, choose, places,
    length, dense_sum, terms, last,
):
    residual, qkv_rows, context, middle, hidden_two, router, gates, record_moe, picked = record
    images, rows, features = gradient.shape
    experts = len(places)
    flat = gradient.reshape(-1, features)
    scaled = [(gates[k] * flat).astype(bf16) for k in range(2)]
    blocks = {}
    for j in sorted(places, reverse=True):
        singles = places[j][1]
        blocks[j] = (dot_on(singles[0], scaled[0], 0, 0) + dot_on(singles[1], scaled[1], 0, 0)).astype(bf16)
    sent = {j: swap(block, "shard", j) if j else block for j, block in blocks.items()}
    grad_two = 0.0
    grad_pres = []
    arriving = []
    partial = expert_grads(after(terms, blocks)) if terms is not None else None
    expert_sum = None
    for group, (_, slope, _) in zip(group_list(), record_moe):
        grad_arrived = jnp.concatenate([sent[j] for j in group], axis=0)
        if partial is not None and not group[0]:
            grad_arrived, partial = lax.optimization_barrier((grad_arrived, partial))
        if dense_sum is not None and group[0]:
            grad_arrived, dense_sum = lax.optimization_barrier((grad_arrived, dense_sum))
            expert_sum = expert_reduce(after(partial, dense_sum))
        grad_act = dot_on(grad_arrived, second_weight, 1, 1)
        grad_pre = (grad_act * slope.astype(f32)).astype(bf16)
        grad_rows = dot_on(grad_pre, first_weight, 1, 1).astype(bf16)
        capacity = grad_rows.shape[0] // len(group)
        back = {}
        for at, j in reversed(list(enumerate(group))):
            block = grad_rows[at * capacity : (at + 1) * capacity]
            back[j] = swap(block, "shard", j) if j else block
        grad_back = jnp.concatenate([back[j] for j in group], axis=0)
        both = jnp.concatenate([places[j][0] for j in group], axis=1)
        grad_two = grad_two + jnp.dot(both, grad_back, preferred_element_type=f32)
        grad_pres.append(grad_pre)
        arriving.append(grad_arrived)
    terms = (grad_pres, [moe[0] for moe in record_moe], [moe[2] for moe in record_moe], arriving)
    last_sum = None
    if last:
        partial = expert_grads(terms)
        grad_two, partial = lax.optimization_barrier((grad_two, partial))
        last_sum = expert_reduce(after(partial, expert_sum))
    grad_router = sum(
        choose[k] * jnp.sum(flat * picked[k].astype(f32), axis=1, keepdims=True) for k in range(2)
    )
    grad_logits = (
        router * (grad_router - jnp.sum(router * grad_router, axis=-1, keepdims=True))
    ).astype(bf16)
    grad_router_w = dot_on(grad_logits, hidden_two, 0, 0)
    grad_two = grad_two + jnp.dot(grad_logits, router_t[:experts], preferred_element_type=f32)
    grad_two = grad_two.reshape(gradient.shape)
    input_grad, grad_weight, norm_sums = attention_backward(
        grad_two, gradient, residual, middle, qkv_rows, context, weight, gains, shifts, length
    )
    items = jnp.concatenate([grad_router_w, norm_sums[:4]], axis=0)
    if expert_sum is not None:
        input_grad, grad_weight, expert_sum = lax.optimization_barrier(
            (input_grad, grad_weight, expert_sum)
        )
    return (input_grad, grad_weight, items, terms, dense_sum, expert_sum, last_sum)


def shards(
    tokens, expert_ids, qkv_weight, out_weight, router_weight, norm_gain, norm_shift, expert_in,
    expert_out, cotangent,
):
    images, length, features = tokens.shape
    padded = -(-length // 16) * 16
    fill = ((0, 0), (0, padded - length), (0, 0))
    experts = lax.axis_size("shard")
    replicas = lax.axis_size("replica")
    token_count = images * length
    capacity = (8 * token_count + 24 * experts - 1) // (24 * experts) * 8
    packed = jnp.concatenate([qkv_weight, out_weight], axis=2)
    router_all = lax.all_gather(
        jnp.transpose(router_weight, (0, 2, 1)).reshape(LAYERS * experts, -1), "shard", axis=1, tiled=True
    ).reshape(LAYERS, experts, features)
    router_all = jnp.pad(router_all, ((0, 0), (0, -experts % 8), (0, 0)))
    weight = lax.all_gather(gather_shard(packed[0]), "replica", axis=0, tiled=False)
    ids_flat = expert_ids.reshape(-1)
    labels = jnp.arange(experts, dtype=jnp.int32)
    member = (ids_flat[:, None] == labels[None, :]).astype(jnp.int32)
    earlier = jnp.cumsum(member, axis=0) - member
    slot = jnp.sum(earlier * member, axis=1).reshape(expert_ids.shape)
    ids_pair = jnp.pad(expert_ids, fill, constant_values=-1).reshape(-1, 2)
    slot = jnp.pad(slot, fill).reshape(-1, 2)
    choose = [(ids_pair[:, k : k + 1] == labels[None, :]).astype(f32) for k in range(2)]
    slot_row = jnp.arange(capacity, dtype=jnp.int32)[None, :]
    places = {}
    for j in range(experts):
        expert = lax.axis_index("shard") ^ j
        at = jnp.where(ids_pair == expert, slot, -1)
        singles = [(at[:, k : k + 1] == slot_row).astype(bf16) for k in range(2)]
        places[j] = (singles[0] + singles[1], singles)
    residual = jnp.pad(tokens, fill).astype(f32)
    records = []
    weights = []
    for index in range(LAYERS):
        weights.append(weight)
        tall = None
        if index + 1 < LAYERS:
            tall = gather_shard(after(packed[index + 1], weight))
        record, residual, weight = forward_layer(
            residual, weight, router_all[index], norm_gain[index], norm_shift[index],
            expert_in[index, 0], expert_out[index, 0], choose, places, length, tall,
        )
        records.append(record)
    activations = residual[:, :length].astype(bf16)
    gradient = jnp.pad(cotangent, fill).astype(f32)
    expert_sums = [None] * LAYERS
    items = [None] * LAYERS
    dense_sums = []
    dense_sum, terms = None, None
    for index in range(LAYERS - 1, -1, -1):
        gradient, grad_weight, items[index], terms, dense_sum, expert_sum, last_sum = backward_layer(
            gradient, records[index], weights[index], router_all[index], norm_gain[index],
            norm_shift[index], expert_in[index, 0], expert_out[index, 0], choose, places, length,
            dense_sum, terms, index == 0,
        )
        if index + 1 < LAYERS:
            expert_sums[index + 1] = expert_sum
            dense_sums.append(dense_sum)
        if index:
            dense_sum = lax.psum_scatter(grad_weight, "replica", scatter_dimension=0, tiled=False)
    expert_sums[0] = last_sum
    upper = lax.psum_scatter(
        after(jnp.concatenate(dense_sums[::-1], axis=1), last_sum), "shard", scatter_dimension=0, tiled=True
    )
    upper = lax.all_gather(upper, "replica", axis=0, tiled=False)
    input_grad = gradient[:, :length]
    rows = features // experts
    width = grad_weight.shape[-1]
    count = items[0].shape[0]
    small = jnp.stack(items, axis=1).astype(bf16).reshape(count, LAYERS, experts, rows)
    small = jnp.pad(
        jnp.transpose(small, (0, 2, 1, 3)), ((0, replicas - count), (0, 0), (0, 8 - LAYERS), (0, width - rows))
    )
    tail = reduce_tail(
        jnp.concatenate([grad_weight.reshape(replicas, experts, rows, width), small], axis=2)
    )
    parts = [tail[:, :rows]] + [upper[:, :, n * width : (n + 1) * width] for n in range(LAYERS - 1)]
    small = tail[:count, rows : rows + LAYERS, :rows].astype(f32)
    qkv_grad, out_grad = assemble(parts, features)
    router_grad = jnp.transpose(small[:experts], (1, 2, 0))
    norm_grads = jnp.transpose(small[experts:], (1, 0, 2))
    gain_grad = norm_grads[:, :2]
    shift_grad = norm_grads[:, 2:]
    expert_sums = [part.reshape(2, -1, features).astype(f32) for part in expert_sums]
    expert_in_grad = jnp.stack([jnp.transpose(part[0])[None] for part in expert_sums])
    expert_out_grad = jnp.stack([part[1][None] for part in expert_sums])
    return (
        activations, input_grad, qkv_grad, out_grad, router_grad, gain_grad, shift_grad,
        expert_in_grad, expert_out_grad,
    )


def solution(mesh):
    in_specs = (
        P(("replica", "shard"), None, None),
        P(("replica", "shard"), None, None),
        P(None, "shard", None),
        P(None, "shard", None),
        P(None, "shard", None),
        P(),
        P(),
        P(None, "shard", None, None),
        P(None, "shard", None, None),
        P(("replica", "shard"), None, None),
    )
    out_specs = (
        P(("replica", "shard"), None, None),
        P(("replica", "shard"), None, None),
        P(None, "shard", None),
        P(None, "shard", None),
        P(None, "shard", None),
        P(None, None, "shard"),
        P(None, None, "shard"),
        P(None, "shard", None, "replica"),
        P(None, "shard", "replica", None),
    )
    return jax.shard_map(shards, mesh=mesh, in_specs=in_specs, out_specs=out_specs, check_vma=False)
```

```python
import functools

import jax
import jax.numpy as jnp
from jax import lax
from jax.experimental import pallas as pl
from jax.experimental.pallas import tpu as pltpu
from jax.sharding import PartitionSpec as P


HEAD = 64
LAYERS = 3

eps_norm = 1e-06
inv_root_two = 0.7071067811865476
inv_root_two_pi = 0.3989422804014327
bf16 = jnp.bfloat16
f32 = jnp.float32


def dot_on(left, right, left_axis, right_axis):
    return lax.dot_general(
        left, right, (((left_axis,), (right_axis,)), ((), ())), preferred_element_type=f32
    )


def swap(values, axis, bit):
    count = lax.axis_size(axis)
    return lax.ppermute(values, axis, [(n, n ^ bit) for n in range(count)])


def bit_of(axis, bit):
    return (lax.axis_index(axis) & bit) != 0


def bits_from(axis, step):
    bits = []
    while step < lax.axis_size(axis):
        bits.append(step)
        step *= 2
    return bits


def orders():
    bits = bits_from("replica", 2)
    return bits, bits[::-1]


def add_swapped(values, axis, bit, size, at):
    lead, rows, rest = values.shape[:at], values.shape[at], values.shape[at + 1 :]
    view = values.reshape(lead + (rows // (2 * size), 2, size) + rest)
    own = bit_of(axis, bit).astype(jnp.int32)
    kept = lax.dynamic_index_in_dim(view, own, at + 1, keepdims=False)
    sent = lax.dynamic_index_in_dim(view, 1 - own, at + 1, keepdims=False)
    shape = lead + (rows // 2,) + rest
    arrived = swap(sent.reshape(shape), axis, bit)
    return (kept.reshape(shape).astype(f32) + arrived.astype(f32)).astype(bf16)


def join_swapped(values, axis, bit, size, at):
    other = swap(values, axis, bit)
    lead, rows, rest = values.shape[:at], values.shape[at], values.shape[at + 1 :]
    shape = lead + (rows // size, size) + rest
    mine, theirs = values.reshape(shape), other.reshape(shape)
    upper = bit_of(axis, bit)
    pair = [jnp.where(upper, theirs, mine), jnp.where(upper, mine, theirs)]
    return jnp.stack(pair, axis=at + 1).reshape(lead + (2 * rows,) + rest)


def size_below(bit, held):
    size = 1
    for other in held:
        if other < bit:
            size *= 2
    return size


def cut(values):
    middle = values.shape[-2] // 16 * 8
    return (values[..., :middle, :], values[..., middle:, :])


def scatter_replica(values, *others):
    values = add_swapped(values, "replica", 1, 1, 1)
    values, *others = lax.optimization_barrier((values,) + others)
    parts = []
    for piece, order in zip(cut(values), orders()):
        for at, bit in enumerate(order):
            piece = add_swapped(piece, "replica", bit, size_below(bit, order[at + 1 :]), 1)
        parts.append(piece[:, 0])
    return jnp.concatenate(parts, axis=-2), others


def gather_replica(values):
    done = []
    for piece, order in zip(cut(values), orders()):
        piece = piece[:, None]
        held = []
        for bit in order[::-1]:
            piece = join_swapped(piece, "replica", bit, size_below(bit, held), 1)
            held.append(bit)
        done.append(piece)
    return join_swapped(jnp.concatenate(done, axis=-2), "replica", 1, 1, 1)


def after(values, *others):
    return lax.optimization_barrier((values,) + others)[0]


def gather_shard(packed):
    rows, columns = packed.shape
    width = columns // lax.axis_size("replica")
    own = lax.dynamic_slice_in_dim(packed, lax.axis_index("replica") * width, width, axis=1)
    shards_ = lax.axis_size("shard")
    spread = jnp.broadcast_to(own[None], (shards_, rows, width))
    tall = lax.all_to_all(spread, "shard", split_axis=0, concat_axis=0, tiled=True)
    return tall.reshape(shards_ * rows, width)


def split_sum(summed, features):
    if isinstance(summed, tuple):
        return summed
    return summed[:, :features], summed[:, features:]


def norm_rows_of(values, features):
    average = jnp.sum(values, axis=-1, keepdims=True) * (1.0 / features)
    centred = values - average
    variance = jnp.sum(centred * centred, axis=-1, keepdims=True) * (1.0 / features)
    inverse = lax.rsqrt(variance + eps_norm)
    return centred * inverse, inverse


def soft_scores(queries, key_rows, length):
    scores = dot_on(queries, key_rows, 1, 1) * HEAD ** (-0.5)
    column = lax.broadcasted_iota(jnp.int32, scores.shape, 1)
    scores = jnp.where(column < length, scores, -1e30)
    raised = jnp.exp(scores - jnp.max(scores, axis=-1, keepdims=True))
    return raised * (1.0 / jnp.sum(raised, axis=-1, keepdims=True))


def attention_kernel(length, res_ref, w_ref, rt_ref, gain_ref, shift_ref, qkv_ref, ctx_ref, mid_ref, hid_ref, log_ref):
    residual = res_ref[0]
    features = residual.shape[1]
    normed, _ = norm_rows_of(residual, features)
    hidden = (normed * gain_ref[0:1] + shift_ref[0:1]).astype(bf16)
    width = w_ref.shape[2]
    inner = 3 * features // width
    for chunk in range(inner):
        qkv_ref[0, :, chunk * width : (chunk + 1) * width] = jnp.dot(
            hidden, w_ref[chunk], preferred_element_type=f32
        ).astype(bf16)
    for pair in range(features // (2 * HEAD)):
        outs = []
        for head in (2 * pair, 2 * pair + 1):
            at = head * HEAD
            queries, key_rows, value_rows = [
                qkv_ref[0, :, part * features + at : part * features + at + HEAD] for part in range(3)
            ]
            weights = soft_scores(queries, key_rows, length).astype(bf16)
            outs.append(jnp.dot(weights, value_rows, preferred_element_type=f32).astype(bf16))
        ctx_ref[0, :, 2 * pair * HEAD : (2 * pair + 2) * HEAD] = jnp.concatenate(outs, axis=1)
    for chunk in range(inner, w_ref.shape[0]):
        at = (chunk - inner) * width
        mid_ref[0, :, at : at + width] = res_ref[0, :, at : at + width] + jnp.dot(
            ctx_ref[0], w_ref[chunk], preferred_element_type=f32
        )
    middle = mid_ref[0]
    normed, _ = norm_rows_of(middle, features)
    hidden = (normed * gain_ref[1:2] + shift_ref[1:2]).astype(bf16)
    hid_ref[0] = hidden
    log_ref[0] = dot_on(hidden, rt_ref[...], 1, 1)


def attention_forward(residual, weight, router_t, gains, shifts, length):
    images, rows, features = residual.shape

    def per_image(width):
        return pl.BlockSpec((1, rows, width), lambda n: (n, 0, 0))

    def whole(shape):
        return pl.BlockSpec(shape, lambda n: (0,) * len(shape), pipeline_mode=pl.Buffered(1))

    extra = router_t.shape[0]
    shape = jax.ShapeDtypeStruct
    return pl.pallas_call(
        functools.partial(attention_kernel, length),
        grid=(images,),
        in_specs=[
            per_image(features), whole(weight.shape), whole(router_t.shape), whole(gains.shape),
            whole(shifts.shape),
        ],
        out_specs=[
            per_image(3 * features), per_image(features), per_image(features), per_image(features),
            per_image(extra),
        ],
        out_shape=[
            shape((images, rows, 3 * features), bf16), shape((images, rows, features), bf16),
            shape((images, rows, features), f32), shape((images, rows, features), bf16),
            shape((images, rows, extra), f32),
        ],
        compiler_params=pltpu.CompilerParams(
            dimension_semantics=("arbitrary",), vmem_limit_bytes=48 * 2**20
        ),
        name="attention_forward",
    )(residual, weight, router_t, gains, shifts)


def norm_back_rows(grad_out, normed, inverse, gain_row, features):
    scaled = grad_out * gain_row
    inner = jnp.sum(scaled, axis=-1, keepdims=True) * (1.0 / features)
    along = jnp.sum(scaled * normed, axis=-1, keepdims=True) * (1.0 / features)
    grad_in = inverse * (scaled - inner - normed * along)
    gain_sum = jnp.sum(grad_out * normed, axis=0, keepdims=True)
    return grad_in, gain_sum, jnp.sum(grad_out, axis=0, keepdims=True)


def attention_back_kernel(
    length, two_ref, grad_ref, res_ref, mid_ref, qkv_ref, ctx_ref, w_ref, gain_ref, shift_ref,
    in_ref, dw_ref, norm_ref, dqkv_ref, sum_ref, norm_sum_ref,
):
    step = pl.program_id(0)
    features = res_ref.shape[2]
    scale = HEAD ** (-0.5)

    @pl.when(step == 0)
    def _():
        sum_ref[...] = jnp.zeros_like(sum_ref)
        norm_sum_ref[...] = jnp.zeros_like(norm_sum_ref)

    normed, inverse = norm_rows_of(mid_ref[0], features)
    grad_in, gain_two, shift_two = norm_back_rows(two_ref[0], normed, inverse, gain_ref[1:2], features)
    grad_middle = grad_ref[0] + grad_in
    in_ref[0] = grad_middle
    grad_attn = grad_middle.astype(bf16)
    width = w_ref.shape[2]
    inner_chunks = 3 * features // width
    grad_context = jnp.zeros(grad_attn.shape, f32)
    for chunk in range(inner_chunks, w_ref.shape[0]):
        at = (chunk - inner_chunks) * width
        part = grad_attn[:, at : at + width]
        sum_ref[chunk] += dot_on(ctx_ref[0], part, 0, 0)
        grad_context += dot_on(part, w_ref[chunk], 1, 1)
    grad_context = grad_context.astype(bf16)
    for pair in range(features // (2 * HEAD)):
        outs = ([], [], [])
        for head in (2 * pair, 2 * pair + 1):
            at = head * HEAD
            queries, key_rows, value_rows = [
                qkv_ref[0, :, part * features + at : part * features + at + HEAD] for part in range(3)
            ]
            grad_head = grad_context[:, at : at + HEAD]
            weights = soft_scores(queries, key_rows, length)
            grad_weights = dot_on(grad_head, value_rows, 1, 1)
            outs[2].append(dot_on(weights.astype(bf16), grad_head, 0, 0))
            inner = jnp.sum(weights * grad_weights, axis=-1, keepdims=True)
            grad_scores = (weights * (grad_weights - inner)).astype(bf16)
            outs[0].append(jnp.dot(grad_scores, key_rows, preferred_element_type=f32) * scale)
            outs[1].append(dot_on(grad_scores, queries, 0, 0) * scale)
        for part in range(3):
            at = part * features + 2 * pair * HEAD
            dqkv_ref[:, at : at + 2 * HEAD] = jnp.concatenate(outs[part], axis=1).astype(bf16)
    normed, inverse = norm_rows_of(res_ref[0], features)
    hidden = (normed * gain_ref[0:1] + shift_ref[0:1]).astype(bf16)
    grad_one = jnp.zeros(normed.shape, f32)
    for chunk in range(inner_chunks):
        part = dqkv_ref[:, chunk * width : (chunk + 1) * width]
        sum_ref[chunk] += dot_on(hidden, part, 0, 0)
        grad_one += dot_on(part, w_ref[chunk], 1, 1)
    grad_in, gain_one, shift_one = norm_back_rows(grad_one, normed, inverse, gain_ref[0:1], features)
    in_ref[0] += grad_in
    for row, value in enumerate((gain_one, gain_two, shift_one, shift_two)):
        norm_sum_ref[row : row + 1] += value

    @pl.when(step == pl.num_programs(0) - 1)
    def _():
        dw_ref[...] = sum_ref[...].astype(bf16)
        norm_ref[...] = norm_sum_ref[...]


def attention_backward(
    grad_two, gradient, residual, middle, qkv_rows, context, weight, gains, shifts, length, wide
):
    images, rows, features = residual.shape

    def per_image(width):
        return pl.BlockSpec((1, rows, width), lambda n: (n, 0, 0))

    def whole(shape):
        return pl.BlockSpec(shape, lambda n: (0,) * len(shape), pipeline_mode=pl.Buffered(1))

    shape = jax.ShapeDtypeStruct
    place = features // weight.shape[2] if wide else 0
    room = weight.shape[:2] + ((place + 1) * weight.shape[2],)
    return pl.pallas_call(
        functools.partial(attention_back_kernel, length),
        grid=(images,),
        in_specs=[per_image(features)] * 4
        + [per_image(3 * features), per_image(features), whole(weight.shape), whole(gains.shape),
           whole(shifts.shape)],
        out_specs=[
            per_image(features),
            pl.BlockSpec(weight.shape, lambda n: (0, 0, place), pipeline_mode=pl.Buffered(1)),
            whole((8, features)),
        ],
        out_shape=[
            shape((images, rows, features), f32), shape(room, bf16),
            shape((8, features), f32),
        ],
        scratch_shapes=[
            pltpu.VMEM((rows, 3 * features), bf16), pltpu.VMEM(weight.shape, f32),
            pltpu.VMEM((8, features), f32),
        ],
        compiler_params=pltpu.CompilerParams(
            dimension_semantics=("arbitrary",), vmem_limit_bytes=56 * 2**20
        ),
        name="attention_backward",
    )(grad_two, gradient, residual, middle, qkv_rows, context, weight, gains, shifts)


def expert_grads(terms, room=None):
    pres, arrived, acts, grads = terms
    groups = len(pres)
    hidden = pres[0].shape[1]
    features = arrived[0].shape[1]
    count = lax.axis_size("replica")
    per = hidden // count
    block = max(per, 384)
    extra = () if room is None else (room,)

    def kernel(*refs):
        out_ref = refs[-1]
        parts = [refs[n * groups : (n + 1) * groups] for n in range(4)]
        for side, (left, right) in enumerate((parts[:2], parts[2:])):
            total = dot_on(left[0][...], right[0][...], 0, 0)
            for n in range(1, groups):
                total += dot_on(left[n][...], right[n][...], 0, 0)
            for n in range(out_ref.shape[0]):
                out_ref[n, side * per : (side + 1) * per] = total[n * per : (n + 1) * per].astype(bf16)

    cut_spec = [pl.BlockSpec((v.shape[0], block), lambda n: (0, n)) for v in pres]
    full_spec = [
        pl.BlockSpec(v.shape, lambda n: (0, 0), pipeline_mode=pl.Buffered(1)) for v in arrived
    ]
    shape = (count, 2 * per, features) if room is None else room.shape
    return pl.pallas_call(
        kernel,
        grid=(hidden // block,),
        in_specs=cut_spec + full_spec + cut_spec + full_spec
        + [pl.BlockSpec(memory_space=pl.ANY)] * len(extra),
        out_specs=pl.BlockSpec((block // per, 2 * per, features), lambda n: (n, 0, 0)),
        out_shape=jax.ShapeDtypeStruct(shape, bf16),
        input_output_aliases={4 * groups: 0} if extra else {},
        compiler_params=pltpu.CompilerParams(
            dimension_semantics=("arbitrary",), vmem_limit_bytes=40 * 2**20
        ),
        name="expert_grads",
    )(*pres, *arrived, *acts, *grads, *extra)


def sum_replica(values):
    return lax.psum_scatter(values, "replica", scatter_dimension=0, tiled=False)


def assemble_experts_kernel(*refs):
    parts, in_ref, out_ref = refs[:-2], refs[-2], refs[-1]
    for layer, part in enumerate(parts):
        per = part.shape[0] // 2
        in_ref[layer, 0] = jnp.transpose(part[:per].astype(f32))
        out_ref[layer, 0] = part[per:].astype(f32)


def assemble_experts(parts):
    rows, features = parts[0].shape
    shape = jax.ShapeDtypeStruct
    return pl.pallas_call(
        assemble_experts_kernel,
        out_shape=[
            shape((len(parts), 1, features, rows // 2), f32),
            shape((len(parts), 1, rows // 2, features), f32),
        ],
        compiler_params=pltpu.CompilerParams(vmem_limit_bytes=40 * 2**20),
        name="assemble_experts",
    )(*parts)


def assemble_kernel(features, starts, rows, part, qkv_ref, out_ref):
    width = part.shape[2]
    inner = 3 * features // width
    for layer, start in enumerate(starts):
        for chunk in range(part.shape[0]):
            values = part[chunk, start : start + rows].astype(f32)
            if chunk < inner:
                qkv_ref[layer, :, chunk * width : (chunk + 1) * width] = values
            else:
                at = (chunk - inner) * width
                out_ref[layer, :, at : at + width] = values


def assemble(tail, features, starts, rows):
    shape = jax.ShapeDtypeStruct
    return pl.pallas_call(
        functools.partial(assemble_kernel, features, starts, rows),
        out_shape=[
            shape((len(starts), rows, 3 * features), f32), shape((len(starts), rows, features), f32)
        ],
        compiler_params=pltpu.CompilerParams(vmem_limit_bytes=40 * 2**20),
        name="assemble",
    )(tail)


def group_list():
    count = lax.axis_size("shard")
    return [list(range(count // 2)), list(range(count // 2, count))]


def expert_forward(arrived, first_weight, second_weight):
    pre_act = jnp.dot(arrived, first_weight, preferred_element_type=f32)
    spread = lax.erf(pre_act * inv_root_two)
    activated = (0.5 * pre_act * (1.0 + spread)).astype(bf16)
    slope = (
        0.5 * (1.0 + spread) + pre_act * jnp.exp(-0.5 * pre_act * pre_act) * inv_root_two_pi
    ).astype(bf16)
    produced = jnp.dot(activated, second_weight, preferred_element_type=f32).astype(bf16)
    return activated, slope, produced


def forward_layer(
    residual, weight, router_t, gains, shifts, first_weight, second_weight, choose, places, length,
    tall,
):
    _, _, features = residual.shape
    experts = len(places)
    qkv_rows, context, middle, hidden_two, logits = attention_forward(
        residual, weight, router_t, gains, shifts, length
    )
    gathered = None
    if tall is not None:
        hidden_two, tall = lax.optimization_barrier((hidden_two, tall))
        gathered = lax.all_gather(tall, "replica", axis=0, tiled=False)
    hidden_two = hidden_two.reshape(-1, features)
    router = jax.nn.softmax(logits.reshape(-1, logits.shape[-1])[:, :experts], axis=-1)
    gates = [jnp.sum(choose[k] * router, axis=1, keepdims=True) for k in range(2)]
    record_moe, picked = [], [0.0, 0.0]
    sent = {}
    for j in sorted(places, reverse=True):
        block = dot_on(places[j][0], hidden_two, 0, 0).astype(bf16)
        sent[j] = swap(block, "shard", j) if j else block
    for group in group_list():
        arrived = jnp.concatenate([sent[j] for j in group], axis=0)
        activated, slope, produced = expert_forward(arrived, first_weight, second_weight)
        capacity = produced.shape[0] // len(group)
        back = {}
        for at, j in reversed(list(enumerate(group))):
            block = produced[at * capacity : (at + 1) * capacity]
            back[j] = swap(block, "shard", j) if j else block
        returned = jnp.concatenate([back[j] for j in group], axis=0)
        for k in range(2):
            single = jnp.concatenate([places[j][1][k] for j in group], axis=1)
            picked[k] = picked[k] + jnp.dot(single, returned, preferred_element_type=f32)
        record_moe.append((arrived, slope, activated))
    mixed = gates[0] * picked[0] + gates[1] * picked[1]
    residual_next = middle + mixed.reshape(middle.shape)
    if gathered is not None:
        residual_next, gathered = lax.optimization_barrier((residual_next, gathered))
    picked = [p.astype(bf16) for p in picked]
    record = (
        residual, qkv_rows, context, middle, hidden_two, router, gates, record_moe, picked,
    )
    return (record, residual_next, gathered)


def backward_layer(
    gradient, record, weight, router_t, gains, shifts, first_weight, second_weight, choose, places,
    length, upper_grad, terms, earlier, last, wide,
):
    residual, qkv_rows, context, middle, hidden_two, router, gates, record_moe, picked = record
    _, _, features = gradient.shape
    experts = len(places)
    flat = gradient.reshape(-1, features)
    scaled = [(gates[k] * flat).astype(bf16) for k in range(2)]
    blocks = {}
    for j in sorted(places, reverse=True):
        singles = places[j][1]
        blocks[j] = (dot_on(singles[0], scaled[0], 0, 0) + dot_on(singles[1], scaled[1], 0, 0)).astype(bf16)
    sent = {}
    for j, block in blocks.items():
        sent[j] = swap(block, "shard", j) if j else block
    grad_two = 0.0
    grad_pres = []
    arriving = []
    summed = None
    if terms is not None:
        terms = after(terms, blocks)
        partial = expert_grads(terms, upper_grad) if wide else (expert_grads(terms), upper_grad)
    for group, (_, slope, _) in zip(group_list(), record_moe):
        grad_arrived = jnp.concatenate([sent[j] for j in group], axis=0)
        if terms is not None and not group[0]:
            grad_arrived, partial, earlier = lax.optimization_barrier((grad_arrived, partial, earlier))
            summed = jax.tree.map(sum_replica, after(partial, earlier))
        grad_act = dot_on(grad_arrived, second_weight, 1, 1)
        grad_pre = (grad_act * slope.astype(f32)).astype(bf16)
        grad_rows = dot_on(grad_pre, first_weight, 1, 1).astype(bf16)
        capacity = grad_rows.shape[0] // len(group)
        back = {}
        for at, j in reversed(list(enumerate(group))):
            block = grad_rows[at * capacity : (at + 1) * capacity]
            back[j] = swap(block, "shard", j) if j else block
        grad_back = jnp.concatenate([back[j] for j in group], axis=0)
        both = jnp.concatenate([places[j][0] for j in group], axis=1)
        grad_two = grad_two + jnp.dot(both, grad_back, preferred_element_type=f32)
        grad_pres.append(grad_pre)
        arriving.append(grad_arrived)
    terms = (grad_pres, [moe[0] for moe in record_moe], [moe[2] for moe in record_moe], arriving)
    own_grads = None
    if last:
        own_grads = expert_grads(terms)
        grad_two, own_grads = lax.optimization_barrier((grad_two, own_grads))
    grad_router = sum(
        choose[k] * jnp.sum(flat * picked[k].astype(f32), axis=1, keepdims=True) for k in range(2)
    )
    grad_logits = (
        router * (grad_router - jnp.sum(router * grad_router, axis=-1, keepdims=True))
    ).astype(bf16)
    grad_router_w = dot_on(grad_logits, hidden_two, 0, 0)
    grad_two = grad_two + jnp.dot(grad_logits, router_t[:experts], preferred_element_type=f32)
    grad_two = grad_two.reshape(gradient.shape)
    input_grad, grad_weight, norm_sums = attention_backward(
        grad_two, gradient, residual, middle, qkv_rows, context, weight, gains, shifts, length,
        wide and not last,
    )
    items = jnp.concatenate([grad_router_w, norm_sums[:4]], axis=0)
    return (input_grad, grad_weight, items, terms, summed, earlier, own_grads)


def shards(
    tokens, expert_ids, qkv_weight, out_weight, router_weight, norm_gain, norm_shift, expert_in,
    expert_out, cotangent,
):
    images, length, features = tokens.shape
    padded = -(-length // 16) * 16
    fill = ((0, 0), (0, padded - length), (0, 0))
    experts = lax.axis_size("shard")
    replicas = lax.axis_size("replica")
    token_count = images * length
    capacity = (8 * token_count + 24 * experts - 1) // (24 * experts) * 8
    packed = jnp.concatenate([qkv_weight, out_weight], axis=2)
    router_all = lax.all_gather(
        jnp.transpose(router_weight, (0, 2, 1)).reshape(LAYERS * experts, -1), "shard", axis=1, tiled=True
    ).reshape(LAYERS, experts, features)
    router_all = jnp.pad(router_all, ((0, 0), (0, -experts % 8), (0, 0)))
    weight = lax.all_gather(gather_shard(packed[0]), "replica", axis=0, tiled=False)
    ids_flat = expert_ids.reshape(-1)
    labels = jnp.arange(experts, dtype=jnp.int32)
    member = (ids_flat[:, None] == labels[None, :]).astype(jnp.int32)
    earlier = jnp.cumsum(member, axis=0) - member
    slot = jnp.sum(earlier * member, axis=1).reshape(expert_ids.shape)
    ids_pair = jnp.pad(expert_ids, fill, constant_values=-1).reshape(-1, 2)
    slot = jnp.pad(slot, fill).reshape(-1, 2)
    choose = [(ids_pair[:, k : k + 1] == labels[None, :]).astype(f32) for k in range(2)]
    slot_row = jnp.arange(capacity, dtype=jnp.int32)[None, :]
    places = {}
    for j in range(experts):
        expert = lax.axis_index("shard") ^ j
        at = jnp.where(ids_pair == expert, slot, -1)
        singles = [(at[:, k : k + 1] == slot_row).astype(bf16) for k in range(2)]
        places[j] = (singles[0] + singles[1], singles)
    residual = jnp.pad(tokens, fill).astype(f32)
    records = []
    weights = []
    for index in range(LAYERS):
        weights.append(weight)
        tall = None
        if index + 1 < LAYERS:
            tall = gather_shard(after(packed[index + 1], weight))
        record, residual, weight = forward_layer(
            residual, weight, router_all[index], norm_gain[index], norm_shift[index],
            expert_in[index, 0], expert_out[index, 0], choose, places, length, tall,
        )
        records.append(record)
    activations = residual[:, :length].astype(bf16)
    gradient = jnp.pad(cotangent, fill).astype(f32)
    items = [None] * LAYERS
    grad_weight, terms, summed = None, None, ()
    wide = 2 * (expert_in.shape[3] // replicas) == features and features % (4 * features // replicas) == 0
    for index in range(LAYERS - 1, -1, -1):
        gradient, grad_weight, items[index], terms, summed, earlier, own_grads = backward_layer(
            gradient, records[index], weights[index], router_all[index], norm_gain[index],
            norm_shift[index], expert_in[index, 0], expert_out[index, 0], choose, places, length,
            grad_weight, terms, () if summed is None else summed, index == 0, wide,
        )
    input_grad = gradient[:, :length]
    rows = features // experts
    width = grad_weight.shape[-1]
    count = items[0].shape[0]
    small = jnp.stack(items, axis=1).astype(bf16).reshape(count, LAYERS, experts, rows)
    small = jnp.pad(
        jnp.transpose(small, (0, 2, 1, 3)), ((0, replicas - count), (0, 0), (0, 8 - LAYERS), (0, width - rows))
    )
    chunks = jnp.concatenate([grad_weight.reshape(replicas, experts, rows, width), small], axis=2)
    whole, (summed, earlier) = scatter_replica(chunks[None], summed, earlier)
    whole = whole[0]
    upper = [split_sum(part, features) for part in (summed, earlier)]
    upper_dense = jnp.concatenate([part[1] for part in upper], axis=1)
    upper_dense = upper_dense.reshape(experts, -1, upper_dense.shape[1])
    for bit in bits_from("shard", 1)[::-1]:
        upper_dense = add_swapped(upper_dense, "shard", bit, bit, 0)
    upper_dense = upper_dense[0]
    own_sum = sum_replica(after(own_grads, summed))
    for bit in bits_from("shard", 1)[::-1]:
        whole = add_swapped(whole, "shard", bit, bit, 0)
    whole = jnp.concatenate(
        [whole[0]] + [upper_dense[:, n * width : (n + 1) * width] for n in range(LAYERS - 1)], axis=0
    )[None]
    expert_in_grad, expert_out_grad = assemble_experts([own_sum] + [part[0] for part in upper])
    whole, expert_in_grad, expert_out_grad = lax.optimization_barrier(
        (whole, expert_in_grad, expert_out_grad)
    )
    tail = gather_replica(whole)[0]
    small = tail[:count, rows : rows + LAYERS, :rows].astype(f32)
    qkv_grad, out_grad = assemble(tail, features, [0, rows + 8, 2 * rows + 8], rows)
    router_grad = jnp.transpose(small[:experts], (1, 2, 0))
    norm_grads = jnp.transpose(small[experts:], (1, 0, 2))
    gain_grad = norm_grads[:, :2]
    shift_grad = norm_grads[:, 2:]
    return (
        activations, input_grad, qkv_grad, out_grad, router_grad, gain_grad, shift_grad,
        expert_in_grad, expert_out_grad,
    )


def solution(mesh):
    in_specs = (
        P(("replica", "shard"), None, None),
        P(("replica", "shard"), None, None),
        P(None, "shard", None),
        P(None, "shard", None),
        P(None, "shard", None),
        P(),
        P(),
        P(None, "shard", None, None),
        P(None, "shard", None, None),
        P(("replica", "shard"), None, None),
    )
    out_specs = (
        P(("replica", "shard"), None, None),
        P(("replica", "shard"), None, None),
        P(None, "shard", None),
        P(None, "shard", None),
        P(None, "shard", None),
        P(None, None, "shard"),
        P(None, None, "shard"),
        P(None, "shard", None, "replica"),
        P(None, "shard", "replica", None),
    )
    return jax.shard_map(shards, mesh=mesh, in_specs=in_specs, out_specs=out_specs, check_vma=False)
```

```python
import functools

import jax
import jax.numpy as jnp
from jax import lax
from jax.experimental import pallas as pl
from jax.experimental.pallas import tpu as pltpu
from jax.sharding import PartitionSpec as P


HEAD = 64
LAYERS = 3

eps_norm = 1e-06
inv_root_two = 0.7071067811865476
inv_root_two_pi = 0.3989422804014327
bf16 = jnp.bfloat16
f32 = jnp.float32


def dot_on(left, right, left_axis, right_axis):
    return lax.dot_general(
        left, right, (((left_axis,), (right_axis,)), ((), ())), preferred_element_type=f32
    )


def swap(values, axis, bit):
    count = lax.axis_size(axis)
    return lax.ppermute(values, axis, [(n, n ^ bit) for n in range(count)])


def bit_of(axis, bit):
    return (lax.axis_index(axis) & bit) != 0


def bits_from(axis, step):
    bits = []
    while step < lax.axis_size(axis):
        bits.append(step)
        step *= 2
    return bits


def orders():
    bits = bits_from("replica", 2)
    return bits, bits[::-1]


def add_swapped(values, axis, bit, size, at, hold=None):
    lead, rows, rest = values.shape[:at], values.shape[at], values.shape[at + 1 :]
    view = values.reshape(lead + (rows // (2 * size), 2, size) + rest)
    own = bit_of(axis, bit).astype(jnp.int32)
    kept = lax.dynamic_index_in_dim(view, own, at + 1, keepdims=False)
    sent = lax.dynamic_index_in_dim(view, 1 - own, at + 1, keepdims=False)
    shape = lead + (rows // 2,) + rest
    arrived = swap(sent.reshape(shape), axis, bit)
    if hold is not None:
        kept = after(kept, hold)
    return (kept.reshape(shape).astype(f32) + arrived.astype(f32)).astype(bf16)


def join_swapped(values, axis, bit, size, at):
    other = swap(values, axis, bit)
    lead, rows, rest = values.shape[:at], values.shape[at], values.shape[at + 1 :]
    shape = lead + (rows // size, size) + rest
    mine, theirs = values.reshape(shape), other.reshape(shape)
    upper = bit_of(axis, bit)
    pair = [jnp.where(upper, theirs, mine), jnp.where(upper, mine, theirs)]
    return jnp.stack(pair, axis=at + 1).reshape(lead + (2 * rows,) + rest)


def size_below(bit, held):
    size = 1
    for other in held:
        if other < bit:
            size *= 2
    return size


def cut(values):
    middle = values.shape[-2] // 16 * 8
    return (values[..., :middle, :], values[..., middle:, :])


def scatter_replica(values, *others):
    values = add_swapped(values, "replica", 1, 1, 1)
    values, *others = lax.optimization_barrier((values,) + others)
    parts = []
    for piece, order in zip(cut(values), orders()):
        for at, bit in enumerate(order):
            piece = add_swapped(piece, "replica", bit, size_below(bit, order[at + 1 :]), 1)
        parts.append(piece[:, 0])
    return jnp.concatenate(parts, axis=-2), others


def gather_replica(values):
    done = []
    for piece, order in zip(cut(values), orders()):
        piece = piece[:, None]
        held = []
        for bit in order[::-1]:
            piece = join_swapped(piece, "replica", bit, size_below(bit, held), 1)
            held.append(bit)
        done.append(piece)
    return join_swapped(jnp.concatenate(done, axis=-2), "replica", 1, 1, 1)


def after(values, *others):
    return lax.optimization_barrier((values,) + others)[0]


def own_columns(packed):
    width = packed.shape[-1] // lax.axis_size("replica")
    return lax.dynamic_slice_in_dim(packed, lax.axis_index("replica") * width, width, axis=packed.ndim - 1)


def gather_shard(own):
    spread = jnp.broadcast_to(own[None], (lax.axis_size("shard"),) + own.shape)
    return lax.all_to_all(spread, "shard", split_axis=0, concat_axis=0, tiled=True)


def split_sum(summed, features):
    if isinstance(summed, tuple):
        return summed
    return summed[:, :features], summed[:, features:]


def norm_rows_of(values, features):
    average = jnp.sum(values, axis=-1, keepdims=True) * (1.0 / features)
    centred = values - average
    variance = jnp.sum(centred * centred, axis=-1, keepdims=True) * (1.0 / features)
    inverse = lax.rsqrt(variance + eps_norm)
    return centred * inverse, inverse


def soft_scores(queries, key_rows, length):
    scores = dot_on(queries, key_rows, 1, 1) * HEAD ** (-0.5)
    column = lax.broadcasted_iota(jnp.int32, scores.shape, 1)
    scores = jnp.where(column < length, scores, -1e30)
    raised = jnp.exp(scores - jnp.max(scores, axis=-1, keepdims=True))
    return raised * (1.0 / jnp.sum(raised, axis=-1, keepdims=True))


def attention_kernel(length, res_ref, w_ref, rt_ref, gain_ref, shift_ref, qkv_ref, ctx_ref, mid_ref, hid_ref, log_ref):
    residual = res_ref[0]
    features = residual.shape[1]
    normed, _ = norm_rows_of(residual, features)
    hidden = (normed * gain_ref[0:1] + shift_ref[0:1]).astype(bf16)
    width = w_ref.shape[2]
    inner = 3 * features // width
    for chunk in range(inner):
        qkv_ref[0, :, chunk * width : (chunk + 1) * width] = jnp.dot(
            hidden, w_ref[chunk], preferred_element_type=f32
        ).astype(bf16)
    for pair in range(features // (2 * HEAD)):
        outs = []
        for head in (2 * pair, 2 * pair + 1):
            at = head * HEAD
            queries, key_rows, value_rows = [
                qkv_ref[0, :, part * features + at : part * features + at + HEAD] for part in range(3)
            ]
            weights = soft_scores(queries, key_rows, length).astype(bf16)
            outs.append(jnp.dot(weights, value_rows, preferred_element_type=f32).astype(bf16))
        ctx_ref[0, :, 2 * pair * HEAD : (2 * pair + 2) * HEAD] = jnp.concatenate(outs, axis=1)
    for chunk in range(inner, w_ref.shape[0]):
        at = (chunk - inner) * width
        mid_ref[0, :, at : at + width] = res_ref[0, :, at : at + width] + jnp.dot(
            ctx_ref[0], w_ref[chunk], preferred_element_type=f32
        )
    middle = mid_ref[0]
    normed, _ = norm_rows_of(middle, features)
    hidden = (normed * gain_ref[1:2] + shift_ref[1:2]).astype(bf16)
    hid_ref[0] = hidden
    log_ref[0] = dot_on(hidden, rt_ref[...], 1, 1)


def attention_forward(residual, weight, router_t, gains, shifts, length):
    images, rows, features = residual.shape

    def per_image(width):
        return pl.BlockSpec((1, rows, width), lambda n: (n, 0, 0))

    def whole(shape):
        return pl.BlockSpec(shape, lambda n: (0,) * len(shape), pipeline_mode=pl.Buffered(1))

    extra = router_t.shape[0]
    shape = jax.ShapeDtypeStruct
    return pl.pallas_call(
        functools.partial(attention_kernel, length),
        grid=(images,),
        in_specs=[
            per_image(features), whole(weight.shape), whole(router_t.shape), whole(gains.shape),
            whole(shifts.shape),
        ],
        out_specs=[
            per_image(3 * features), per_image(features), per_image(features), per_image(features),
            per_image(extra),
        ],
        out_shape=[
            shape((images, rows, 3 * features), bf16), shape((images, rows, features), bf16),
            shape((images, rows, features), f32), shape((images, rows, features), bf16),
            shape((images, rows, extra), f32),
        ],
        compiler_params=pltpu.CompilerParams(
            dimension_semantics=("arbitrary",), vmem_limit_bytes=48 * 2**20
        ),
        name="attention_forward",
    )(residual, weight, router_t, gains, shifts)


def norm_back_rows(grad_out, normed, inverse, gain_row, features):
    scaled = grad_out * gain_row
    inner = jnp.sum(scaled, axis=-1, keepdims=True) * (1.0 / features)
    along = jnp.sum(scaled * normed, axis=-1, keepdims=True) * (1.0 / features)
    grad_in = inverse * (scaled - inner - normed * along)
    gain_sum = jnp.sum(grad_out * normed, axis=0, keepdims=True)
    return grad_in, gain_sum, jnp.sum(grad_out, axis=0, keepdims=True)


def attention_back_kernel(
    length, two_ref, grad_ref, res_ref, mid_ref, qkv_ref, ctx_ref, w_ref, gain_ref, shift_ref,
    in_ref, dw_ref, norm_ref, dqkv_ref, sum_ref, norm_sum_ref,
):
    step = pl.program_id(0)
    features = res_ref.shape[2]
    scale = HEAD ** (-0.5)

    @pl.when(step == 0)
    def _():
        sum_ref[...] = jnp.zeros_like(sum_ref)
        norm_sum_ref[...] = jnp.zeros_like(norm_sum_ref)

    normed, inverse = norm_rows_of(mid_ref[0], features)
    grad_in, gain_two, shift_two = norm_back_rows(two_ref[0], normed, inverse, gain_ref[1:2], features)
    grad_middle = grad_ref[0] + grad_in
    in_ref[0] = grad_middle
    grad_attn = grad_middle.astype(bf16)
    width = w_ref.shape[2]
    inner_chunks = 3 * features // width
    grad_context = jnp.zeros(grad_attn.shape, f32)
    for chunk in range(inner_chunks, w_ref.shape[0]):
        at = (chunk - inner_chunks) * width
        part = grad_attn[:, at : at + width]
        sum_ref[chunk] += dot_on(ctx_ref[0], part, 0, 0)
        grad_context += dot_on(part, w_ref[chunk], 1, 1)
    grad_context = grad_context.astype(bf16)
    for pair in range(features // (2 * HEAD)):
        outs = ([], [], [])
        for head in (2 * pair, 2 * pair + 1):
            at = head * HEAD
            queries, key_rows, value_rows = [
                qkv_ref[0, :, part * features + at : part * features + at + HEAD] for part in range(3)
            ]
            grad_head = grad_context[:, at : at + HEAD]
            weights = soft_scores(queries, key_rows, length)
            grad_weights = dot_on(grad_head, value_rows, 1, 1)
            outs[2].append(dot_on(weights.astype(bf16), grad_head, 0, 0))
            inner = jnp.sum(weights * grad_weights, axis=-1, keepdims=True)
            grad_scores = (weights * (grad_weights - inner)).astype(bf16)
            outs[0].append(jnp.dot(grad_scores, key_rows, preferred_element_type=f32) * scale)
            outs[1].append(dot_on(grad_scores, queries, 0, 0) * scale)
        for part in range(3):
            at = part * features + 2 * pair * HEAD
            dqkv_ref[:, at : at + 2 * HEAD] = jnp.concatenate(outs[part], axis=1).astype(bf16)
    normed, inverse = norm_rows_of(res_ref[0], features)
    hidden = (normed * gain_ref[0:1] + shift_ref[0:1]).astype(bf16)
    grad_one = jnp.zeros(normed.shape, f32)
    for chunk in range(inner_chunks):
        part = dqkv_ref[:, chunk * width : (chunk + 1) * width]
        sum_ref[chunk] += dot_on(hidden, part, 0, 0)
        grad_one += dot_on(part, w_ref[chunk], 1, 1)
    grad_in, gain_one, shift_one = norm_back_rows(grad_one, normed, inverse, gain_ref[0:1], features)
    in_ref[0] += grad_in
    for row, value in enumerate((gain_one, gain_two, shift_one, shift_two)):
        norm_sum_ref[row : row + 1] += value

    @pl.when(step == pl.num_programs(0) - 1)
    def _():
        dw_ref[...] = sum_ref[...].astype(bf16)
        norm_ref[...] = norm_sum_ref[...]


def attention_backward(
    grad_two, gradient, residual, middle, qkv_rows, context, weight, gains, shifts, length, wide
):
    images, rows, features = residual.shape

    def per_image(width):
        return pl.BlockSpec((1, rows, width), lambda n: (n, 0, 0))

    def whole(shape):
        return pl.BlockSpec(shape, lambda n: (0,) * len(shape), pipeline_mode=pl.Buffered(1))

    shape = jax.ShapeDtypeStruct
    place = features // weight.shape[2] if wide else 0
    room = weight.shape[:2] + ((place + 1) * weight.shape[2],)
    return pl.pallas_call(
        functools.partial(attention_back_kernel, length),
        grid=(images,),
        in_specs=[per_image(features)] * 4
        + [per_image(3 * features), per_image(features), whole(weight.shape), whole(gains.shape),
           whole(shifts.shape)],
        out_specs=[
            per_image(features),
            pl.BlockSpec(weight.shape, lambda n: (0, 0, place), pipeline_mode=pl.Buffered(1)),
            whole((8, features)),
        ],
        out_shape=[
            shape((images, rows, features), f32), shape(room, bf16),
            shape((8, features), f32),
        ],
        scratch_shapes=[
            pltpu.VMEM((rows, 3 * features), bf16), pltpu.VMEM(weight.shape, f32),
            pltpu.VMEM((8, features), f32),
        ],
        compiler_params=pltpu.CompilerParams(
            dimension_semantics=("arbitrary",), vmem_limit_bytes=56 * 2**20
        ),
        name="attention_backward",
    )(grad_two, gradient, residual, middle, qkv_rows, context, weight, gains, shifts)


def expert_grads(terms, room=None):
    pres, arrived, acts, grads = terms
    groups = len(pres)
    hidden = pres[0].shape[1]
    features = arrived[0].shape[1]
    count = lax.axis_size("replica")
    per = hidden // count
    block = max(per, 384)
    extra = () if room is None else (room,)

    def kernel(*refs):
        out_ref = refs[-1]
        parts = [refs[n * groups : (n + 1) * groups] for n in range(4)]
        for side, (left, right) in enumerate((parts[:2], parts[2:])):
            total = dot_on(left[0][...], right[0][...], 0, 0)
            for n in range(1, groups):
                total += dot_on(left[n][...], right[n][...], 0, 0)
            for n in range(out_ref.shape[0]):
                out_ref[n, side * per : (side + 1) * per] = total[n * per : (n + 1) * per].astype(bf16)

    cut_spec = [pl.BlockSpec((v.shape[0], block), lambda n: (0, n)) for v in pres]
    full_spec = [
        pl.BlockSpec(v.shape, lambda n: (0, 0), pipeline_mode=pl.Buffered(1)) for v in arrived
    ]
    shape = (count, 2 * per, features) if room is None else room.shape
    return pl.pallas_call(
        kernel,
        grid=(hidden // block,),
        in_specs=cut_spec + full_spec + cut_spec + full_spec
        + [pl.BlockSpec(memory_space=pl.ANY)] * len(extra),
        out_specs=pl.BlockSpec((block // per, 2 * per, features), lambda n: (n, 0, 0)),
        out_shape=jax.ShapeDtypeStruct(shape, bf16),
        input_output_aliases={4 * groups: 0} if extra else {},
        compiler_params=pltpu.CompilerParams(
            dimension_semantics=("arbitrary",), vmem_limit_bytes=40 * 2**20
        ),
        name="expert_grads",
    )(*pres, *arrived, *acts, *grads, *extra)


def sum_replica(values):
    return lax.psum_scatter(values, "replica", scatter_dimension=0, tiled=False)


def assemble_experts_kernel(*refs):
    parts, in_ref, out_ref = refs[:-2], refs[-2], refs[-1]
    for layer, part in enumerate(parts):
        per = part.shape[0] // 2
        in_ref[layer, 0] = jnp.transpose(part[:per].astype(f32))
        out_ref[layer, 0] = part[per:].astype(f32)


def assemble_experts(parts):
    rows, features = parts[0].shape
    shape = jax.ShapeDtypeStruct
    return pl.pallas_call(
        assemble_experts_kernel,
        out_shape=[
            shape((len(parts), 1, features, rows // 2), f32),
            shape((len(parts), 1, rows // 2, features), f32),
        ],
        compiler_params=pltpu.CompilerParams(vmem_limit_bytes=40 * 2**20),
        name="assemble_experts",
    )(*parts)


def assemble_kernel(features, starts, rows, part, qkv_ref, out_ref):
    width = part.shape[2]
    inner = 3 * features // width
    for layer, start in enumerate(starts):
        for chunk in range(part.shape[0]):
            values = part[chunk, start : start + rows].astype(f32)
            if chunk < inner:
                qkv_ref[layer, :, chunk * width : (chunk + 1) * width] = values
            else:
                at = (chunk - inner) * width
                out_ref[layer, :, at : at + width] = values


def assemble(tail, features, starts, rows):
    shape = jax.ShapeDtypeStruct
    return pl.pallas_call(
        functools.partial(assemble_kernel, features, starts, rows),
        out_shape=[
            shape((len(starts), rows, 3 * features), f32), shape((len(starts), rows, features), f32)
        ],
        compiler_params=pltpu.CompilerParams(vmem_limit_bytes=40 * 2**20),
        name="assemble",
    )(tail)


def group_list():
    count = lax.axis_size("shard")
    return [list(range(count // 2)), list(range(count // 2, count))]


def expert_forward(arrived, first_weight, second_weight):
    pre_act = jnp.dot(arrived, first_weight, preferred_element_type=f32)
    spread = lax.erf(pre_act * inv_root_two)
    activated = (0.5 * pre_act * (1.0 + spread)).astype(bf16)
    slope = (
        0.5 * (1.0 + spread) + pre_act * jnp.exp(-0.5 * pre_act * pre_act) * inv_root_two_pi
    ).astype(bf16)
    produced = jnp.dot(activated, second_weight, preferred_element_type=f32).astype(bf16)
    return activated, slope, produced


def forward_layer(
    residual, weight, router_t, gains, shifts, first_weight, second_weight, choose, places, length,
    tall,
):
    _, _, features = residual.shape
    experts = len(places)
    qkv_rows, context, middle, hidden_two, logits = attention_forward(
        residual, weight, router_t, gains, shifts, length
    )
    gathered = None
    if tall is not None:
        hidden_two, tall = lax.optimization_barrier((hidden_two, tall))
        gathered = lax.all_gather(tall, "replica", axis=0, tiled=False)
    hidden_two = hidden_two.reshape(-1, features)
    router = jax.nn.softmax(logits.reshape(-1, logits.shape[-1])[:, :experts], axis=-1)
    gates = [jnp.sum(choose[k] * router, axis=1, keepdims=True) for k in range(2)]
    record_moe, picked = [], [0.0, 0.0]
    sent = {}
    for j in sorted(places, reverse=True):
        block = dot_on(places[j][0], hidden_two, 0, 0).astype(bf16)
        sent[j] = swap(block, "shard", j) if j else block
    for group in group_list():
        arrived = jnp.concatenate([sent[j] for j in group], axis=0)
        activated, slope, produced = expert_forward(arrived, first_weight, second_weight)
        capacity = produced.shape[0] // len(group)
        back = {}
        for at, j in reversed(list(enumerate(group))):
            block = produced[at * capacity : (at + 1) * capacity]
            back[j] = swap(block, "shard", j) if j else block
        returned = jnp.concatenate([back[j] for j in group], axis=0)
        for k in range(2):
            single = jnp.concatenate([places[j][1][k] for j in group], axis=1)
            picked[k] = picked[k] + jnp.dot(single, returned, preferred_element_type=f32)
        record_moe.append((arrived, slope, activated))
    mixed = gates[0] * picked[0] + gates[1] * picked[1]
    residual_next = middle + mixed.reshape(middle.shape)
    if gathered is not None:
        residual_next, gathered = lax.optimization_barrier((residual_next, gathered))
    picked = [p.astype(bf16) for p in picked]
    record = (
        residual, qkv_rows, context, middle, hidden_two, router, gates, record_moe, picked,
    )
    return (record, residual_next, gathered)


def backward_layer(
    gradient, record, weight, router_t, gains, shifts, first_weight, second_weight, choose, places,
    length, upper_grad, terms, earlier, last, wide,
):
    residual, qkv_rows, context, middle, hidden_two, router, gates, record_moe, picked = record
    _, _, features = gradient.shape
    experts = len(places)
    flat = gradient.reshape(-1, features)
    scaled = [(gates[k] * flat).astype(bf16) for k in range(2)]
    blocks = {}
    for j in sorted(places, reverse=True):
        singles = places[j][1]
        blocks[j] = (dot_on(singles[0], scaled[0], 0, 0) + dot_on(singles[1], scaled[1], 0, 0)).astype(bf16)
    sent = {}
    for j, block in blocks.items():
        sent[j] = swap(block, "shard", j) if j else block
    grad_two = 0.0
    grad_pres = []
    arriving = []
    summed = None
    if terms is not None:
        terms = after(terms, blocks)
        partial = expert_grads(terms, upper_grad) if wide else (expert_grads(terms), upper_grad)
    for group, (_, slope, _) in zip(group_list(), record_moe):
        grad_arrived = jnp.concatenate([sent[j] for j in group], axis=0)
        if terms is not None and not group[0]:
            grad_arrived, partial, earlier = lax.optimization_barrier((grad_arrived, partial, earlier))
            summed = jax.tree.map(sum_replica, after(partial, earlier))
        grad_act = dot_on(grad_arrived, second_weight, 1, 1)
        grad_pre = (grad_act * slope.astype(f32)).astype(bf16)
        grad_rows = dot_on(grad_pre, first_weight, 1, 1).astype(bf16)
        capacity = grad_rows.shape[0] // len(group)
        back = {}
        for at, j in reversed(list(enumerate(group))):
            block = grad_rows[at * capacity : (at + 1) * capacity]
            back[j] = swap(block, "shard", j) if j else block
        grad_back = jnp.concatenate([back[j] for j in group], axis=0)
        both = jnp.concatenate([places[j][0] for j in group], axis=1)
        grad_two = grad_two + jnp.dot(both, grad_back, preferred_element_type=f32)
        grad_pres.append(grad_pre)
        arriving.append(grad_arrived)
    terms = (grad_pres, [moe[0] for moe in record_moe], [moe[2] for moe in record_moe], arriving)
    own_grads = None
    if last:
        own_grads = expert_grads(terms)
        grad_two, own_grads = lax.optimization_barrier((grad_two, own_grads))
    grad_router = sum(
        choose[k] * jnp.sum(flat * picked[k].astype(f32), axis=1, keepdims=True) for k in range(2)
    )
    grad_logits = (
        router * (grad_router - jnp.sum(router * grad_router, axis=-1, keepdims=True))
    ).astype(bf16)
    grad_router_w = dot_on(grad_logits, hidden_two, 0, 0)
    grad_two = grad_two + jnp.dot(grad_logits, router_t[:experts], preferred_element_type=f32)
    grad_two = grad_two.reshape(gradient.shape)
    input_grad, grad_weight, norm_sums = attention_backward(
        grad_two, gradient, residual, middle, qkv_rows, context, weight, gains, shifts, length,
        wide and not last,
    )
    items = jnp.concatenate([grad_router_w, norm_sums[:4]], axis=0)
    return (input_grad, grad_weight, items, terms, summed, earlier, own_grads)


def shards(
    tokens, expert_ids, qkv_weight, out_weight, router_weight, norm_gain, norm_shift, expert_in,
    expert_out, cotangent,
):
    images, length, features = tokens.shape
    padded = -(-length // 16) * 16
    fill = ((0, 0), (0, padded - length), (0, 0))
    experts = lax.axis_size("shard")
    replicas = lax.axis_size("replica")
    token_count = images * length
    capacity = (8 * token_count + 24 * experts - 1) // (24 * experts) * 8
    packed = jnp.concatenate([qkv_weight, out_weight], axis=2)
    router_all = lax.all_gather(
        jnp.transpose(router_weight, (0, 2, 1)).reshape(LAYERS * experts, -1), "shard", axis=1, tiled=True
    ).reshape(LAYERS, experts, features)
    router_all = jnp.pad(router_all, ((0, 0), (0, -experts % 8), (0, 0)))
    own = own_columns(packed)
    first = gather_shard(own[0]).reshape(features, -1)
    later = gather_shard(after(own[1:], first))
    weight = lax.all_gather(first, "replica", axis=0, tiled=False)
    ids_flat = expert_ids.reshape(-1)
    labels = jnp.arange(experts, dtype=jnp.int32)
    member = (ids_flat[:, None] == labels[None, :]).astype(jnp.int32)
    earlier = jnp.cumsum(member, axis=0) - member
    slot = jnp.sum(earlier * member, axis=1).reshape(expert_ids.shape)
    ids_pair = jnp.pad(expert_ids, fill, constant_values=-1).reshape(-1, 2)
    slot = jnp.pad(slot, fill).reshape(-1, 2)
    choose = [(ids_pair[:, k : k + 1] == labels[None, :]).astype(f32) for k in range(2)]
    slot_row = jnp.arange(capacity, dtype=jnp.int32)[None, :]
    places = {}
    for j in range(experts):
        expert = lax.axis_index("shard") ^ j
        at = jnp.where(ids_pair == expert, slot, -1)
        singles = [(at[:, k : k + 1] == slot_row).astype(bf16) for k in range(2)]
        places[j] = (singles[0] + singles[1], singles)
    residual = jnp.pad(tokens, fill).astype(f32)
    gradient = jnp.pad(cotangent, fill).astype(f32)
    weight, later, places, choose, gradient = lax.optimization_barrier(
        (weight, later, places, choose, gradient)
    )
    records = []
    weights = []
    for index in range(LAYERS):
        weights.append(weight)
        tall = None
        if index + 1 < LAYERS:
            tall = later[:, index].reshape(features, -1)
        record, residual, weight = forward_layer(
            residual, weight, router_all[index], norm_gain[index], norm_shift[index],
            expert_in[index, 0], expert_out[index, 0], choose, places, length, tall,
        )
        records.append(record)
    activations = residual[:, :length].astype(bf16)
    items = [None] * LAYERS
    grad_weight, terms, summed = None, None, ()
    wide = 2 * (expert_in.shape[3] // replicas) == features and features % (4 * features // replicas) == 0
    for index in range(LAYERS - 1, -1, -1):
        gradient, grad_weight, items[index], terms, summed, earlier, own_grads = backward_layer(
            gradient, records[index], weights[index], router_all[index], norm_gain[index],
            norm_shift[index], expert_in[index, 0], expert_out[index, 0], choose, places, length,
            grad_weight, terms, () if summed is None else summed, index == 0, wide,
        )
    input_grad = gradient[:, :length]
    rows = features // experts
    width = grad_weight.shape[-1]
    count = items[0].shape[0]
    small = jnp.stack(items, axis=1).astype(bf16).reshape(count, LAYERS, experts, rows)
    small = jnp.pad(
        jnp.transpose(small, (0, 2, 1, 3)), ((0, replicas - count), (0, 0), (0, 8 - LAYERS), (0, width - rows))
    )
    chunks = jnp.concatenate([grad_weight.reshape(replicas, experts, rows, width), small], axis=2)
    whole, (summed, earlier) = scatter_replica(chunks[None], summed, earlier)
    whole = whole[0]
    upper = [split_sum(part, features) for part in (summed, earlier)]
    upper_dense = jnp.concatenate([part[1] for part in upper], axis=1)
    upper_dense = upper_dense.reshape(experts, -1, upper_dense.shape[1])
    for bit in bits_from("shard", 1)[::-1]:
        upper_dense = add_swapped(upper_dense, "shard", bit, bit, 0, whole)
    upper_dense = upper_dense[0]
    own_sum = sum_replica(after(own_grads, summed))
    for bit in bits_from("shard", 1)[::-1]:
        whole = add_swapped(whole, "shard", bit, bit, 0)
    whole = jnp.concatenate(
        [whole[0]] + [upper_dense[:, n * width : (n + 1) * width] for n in range(LAYERS - 1)], axis=0
    )[None]
    expert_in_grad, expert_out_grad = assemble_experts([own_sum] + [part[0] for part in upper])
    whole, expert_in_grad, expert_out_grad = lax.optimization_barrier(
        (whole, expert_in_grad, expert_out_grad)
    )
    tail = gather_replica(whole)[0]
    small = tail[:count, rows : rows + LAYERS, :rows].astype(f32)
    qkv_grad, out_grad = assemble(tail, features, [0, rows + 8, 2 * rows + 8], rows)
    router_grad = jnp.transpose(small[:experts], (1, 2, 0))
    norm_grads = jnp.transpose(small[experts:], (1, 0, 2))
    gain_grad = norm_grads[:, :2]
    shift_grad = norm_grads[:, 2:]
    return (
        activations, input_grad, qkv_grad, out_grad, router_grad, gain_grad, shift_grad,
        expert_in_grad, expert_out_grad,
    )


def solution(mesh):
    in_specs = (
        P(("replica", "shard"), None, None),
        P(("replica", "shard"), None, None),
        P(None, "shard", None),
        P(None, "shard", None),
        P(None, "shard", None),
        P(),
        P(),
        P(None, "shard", None, None),
        P(None, "shard", None, None),
        P(("replica", "shard"), None, None),
    )
    out_specs = (
        P(("replica", "shard"), None, None),
        P(("replica", "shard"), None, None),
        P(None, "shard", None),
        P(None, "shard", None),
        P(None, "shard", None),
        P(None, None, "shard"),
        P(None, None, "shard"),
        P(None, "shard", None, "replica"),
        P(None, "shard", "replica", None),
    )
    return jax.shard_map(shards, mesh=mesh, in_specs=in_specs, out_specs=out_specs, check_vma=False)
```
